128 devices in a mesh: row: 32 (over x, z, core), col: 4 (over y).
Axes of the slice: x: 4, y: 4, z: 4, core: 2. Of those that a mesh axis runs over, the one named last changes fastest.
Arguments:
- tile_u: bfloat16 [64, 8, 1024, 128], P('row', 'col'), may hold values from -6 to 6
- tile_v: bfloat16 [64, 8, 128, 1024], P('row', 'col'), may hold values from -0.5 to 0.5
- tile_ranks: int32 [64, 8], P('row', 'col'), may hold values from 32 to 128
- inverses: bfloat16 [2, 1024, 1024], replicated, may hold values from -0.005859375 to 0.005859375
- panel_order: int32 [2, 2], replicated, may hold values from 0 to 63, as said below
Outputs:
- trailing: bfloat16 [64, 8, 1024, 1024], P('row', 'col')
The draws below stay inside these ranges and needn't reach their ends.
Inputs may be any that keep to these rules, and one draw needn't show every extreme that they name: `panel_order`: column 0 names 2 different tile rows, below 64; column 1 names 2 different tile columns, below 8; the last tile row and the last tile column are always among them.
All inputs are finite; a program needn't handle non-finite values.
Results may differ from the reference program's by a relative error of at most 0.0075.
Values may be sent and summed in bfloat16 or wider, within the bound.
A program may use at most 128 MiB of HBM per device.

```python
import jax
import jax.numpy as jnp
from jax import lax

B = 1024
RK = 128
STEPS = 2
TILE_ROWS = 64
TILE_COLS = 8


def pick_with_last(key, count):
    earlier = jax.random.permutation(jax.random.fold_in(key, 1), count - 1)[:STEPS - 1].astype(jnp.int32)
    joined = jnp.concatenate([earlier, jnp.full((1,), count - 1, dtype=jnp.int32)])
    return jax.random.permutation(jax.random.fold_in(key, 2), joined)


def draw_panel_order(key, part):
    row_pick = pick_with_last(jax.random.fold_in(key, 11), TILE_ROWS)
    column_pick = pick_with_last(jax.random.fold_in(key, 12), TILE_COLS)
    return jnp.stack([row_pick, column_pick], axis=1).astype(jnp.int32)


def with_ends(values, key, low, high):
    longest = values.shape.index(max(values.shape))
    spots = []
    for shift in (0, 1):
        where = [jax.random.randint(jax.random.fold_in(key, axis), (), 0, length) for axis, length in enumerate(values.shape)]
        where[longest] = (where[longest] + shift) % values.shape[longest]
        spots.append(tuple(where))
    return values.at[spots[0]].set(low).at[spots[1]].set(high)


def block_levels(key, dims, split, least, top_value):
    level, own = 1.0, jax.random.fold_in(key, 6)
    for dim, parts in split:
        heights = jnp.exp(jax.random.uniform(jax.random.fold_in(own, dim), (parts,), jnp.float32, least / len(split), top_value / len(split)))
        level = level * jnp.repeat(heights, dims[dim] // parts).reshape([-1 if axis == dim else 1 for axis in range(len(dims))])
    return level


def gaussian(own_key, shape, scale, reach, shards=(), kind=jnp.bfloat16):
    drawn = scale * jax.random.normal(own_key, shape, jnp.float32)
    if shards:
        drawn = drawn * block_levels(own_key, shape, shards, -0.22, 0.18)
    return jnp.clip(drawn, -reach, reach).astype(kind)


def setup_inputs(seed: int = 0) -> dict:
    splits = jax.random.split(jax.random.key(seed), 6)
    return {
        "tile_u": gaussian(splits[0], (TILE_ROWS, TILE_COLS, B, RK), 1.0, 6.0, ((0, 32), (1, 4))),
        "tile_v": gaussian(splits[1], (TILE_ROWS, TILE_COLS, RK, B), RK ** -0.5, 0.5, ((0, 32), (1, 4))),
        "tile_ranks": with_ends(jax.random.randint(splits[2], (TILE_ROWS, TILE_COLS), RK // 4, RK + 1), jax.random.fold_in(splits[2], 1), RK // 4, RK).astype(jnp.int32),
        "inverses": gaussian(splits[3], (STEPS, B, B), (B * B) ** -0.5, 0.005859375),
        "panel_order": draw_panel_order(jax.random.fold_in(splits[5], 71), 0),
    }


def reference(tile_u, tile_v, tile_ranks, inverses, panel_order):
    kept_rows = (jnp.arange(RK, dtype=jnp.int32)[None, None, :] < tile_ranks[:, :, None]).astype(tile_v.dtype)
    left_factors = tile_u
    right_factors = tile_v * kept_rows[..., None]
    row_global = jnp.arange(TILE_ROWS, dtype=jnp.int32)
    column_global = jnp.arange(TILE_COLS, dtype=jnp.int32)
    row_done = jnp.zeros((TILE_ROWS,), dtype=jnp.bool_)
    column_done = jnp.zeros((TILE_COLS,), dtype=jnp.bool_)
    for step_index in range(STEPS):
        pivot_row = panel_order[step_index, 0]
        pivot_column = panel_order[step_index, 1]
        row_done = jnp.logical_or(row_done, row_global == pivot_row)
        column_done = jnp.logical_or(column_done, column_global == pivot_column)
        update_mask = jnp.logical_and(jnp.logical_not(row_done)[:, None], jnp.logical_not(column_done)[None, :]).astype(jnp.float32)
        column_left = lax.dynamic_index_in_dim(left_factors, pivot_column, 1, keepdims=False)
        column_right = lax.dynamic_index_in_dim(right_factors, pivot_column, 1, keepdims=False)
        pivot_left = lax.dynamic_index_in_dim(left_factors, pivot_row, 0, keepdims=False)
        pivot_right = lax.dynamic_index_in_dim(right_factors, pivot_row, 0, keepdims=False)
        solved = jnp.einsum("bd,cdk->cbk", inverses[step_index].astype(jnp.float32), pivot_left.astype(jnp.float32), precision=lax.Precision.HIGHEST).astype(jnp.bfloat16)
        core_block = jnp.einsum("rkb,cbs->rcks", column_right.astype(jnp.float32), solved.astype(jnp.float32), precision=lax.Precision.HIGHEST)
        core_block = core_block.astype(jnp.bfloat16)
        pivot_wide = pivot_right.astype(jnp.float32)

        def update_row(pair_rows):
            core_row, mask_row = pair_rows
            joined = jnp.einsum("cks,csb->ckb", core_row.astype(jnp.float32), pivot_wide)
            return (joined * (-mask_row)[:, None, None]).astype(jnp.bfloat16)

        update = lax.map(update_row, (core_block, update_mask))
        spread = jnp.broadcast_to(column_left[:, None], (TILE_ROWS, TILE_COLS) + column_left.shape[1:])
        left_factors = jnp.concatenate([left_factors, spread], axis=3)
        right_factors = jnp.concatenate([right_factors, update], axis=2)

    def form_row(pair_rows):
        left_row, right_row = pair_rows
        return jnp.einsum("cbk,ckd->cbd", left_row.astype(jnp.float32), right_row.astype(jnp.float32)).astype(jnp.bfloat16)

    return lax.map(form_row, (left_factors, right_factors))
```

```python
import functools

import jax
import jax.numpy as jnp
from jax import lax
from jax.experimental import pallas as pl
from jax.experimental.pallas import tpu as pltpu
from jax.sharding import PartitionSpec as P

MESH = pl.DeviceIdType.MESH
BF = jnp.bfloat16
F32 = jnp.float32
NX = NZ = NY = 4
FIXED_ROW = 31
FIXED_COL = 3
CHUNKS = 2


def column_routes(root_d):
    if root_d == FIXED_COL:
        up, down = [(3, 0), (0, 1), (1, 2)], [(3, 2), (2, 1), (1, 0)]
        return [[up, down], [up, down]]
    if root_d == 1:
        fixed = [[(3, 0), (3, 2), (0, 1)], [(3, 0), (3, 2), (2, 1)]]
        other = [[(1, 2), (1, 0), (2, 3)], [(1, 2), (1, 0), (0, 3)]]
        return [fixed, other]
    if root_d == 0:
        fixed, other = [(3, 0), (3, 2), (2, 1)], [(0, 1), (0, 3), (1, 2)]
    else:
        fixed, other = [(3, 0), (3, 2), (0, 1)], [(2, 1), (2, 3), (1, 0)]
    return [[fixed, fixed], [other, other]]


class Kind:
    def __init__(self, left, src, a, b, core, send1, r1, c2, s2, q3, s3, big, ssem, rsem):
        self.left, self.src, self.a, self.b, self.core = left, src, a, b, core
        self.send1, self.r1, self.c2, self.s2, self.q3, self.s3, self.big = send1, r1, c2, s2, q3, s3, big
        self.ssem, self.rsem = ssem, rsem

    def row_of(self, a, b, core):
        return 8 * a + 2 * b + core if self.left else 2 * a + 8 * b + core

    def quarter(self, k):
        if self.left:
            return (pl.ds(pl.multiple_of(256 * k, 256), 256), slice(None))
        return (pl.ds(pl.multiple_of(32 * k, 32), 32), slice(None))

    def sub(self, k):
        if self.left:
            return (pl.ds(pl.multiple_of(64 * k, 64), 64), slice(None))
        return (slice(None), pl.ds(pl.multiple_of(256 * k, 256), 256))

    def piece(self, a, b):
        if self.left:
            return (pl.ds(pl.multiple_of(256 * a + 64 * b, 64), 64), slice(None))
        return (pl.ds(pl.multiple_of(32 * a, 32), 32), pl.ds(pl.multiple_of(256 * b, 256), 256))


def comm_kernel(root_d, order_ref, ranks_ref, u_hbm, v_hbm, inv_hbm, colu_hbm, x_hbm,
                u, v, inv, vd, ud, colv,
                send1_u, r1_u, c2_u, s2_u, q3_u, s3_u, big_u,
                send1_v, r1_v, c2_v, s2_v, q3_v, s3_v, big_v,
                ucat, s1, s2, vcat, pm1, pm2, rhs1, rhs2, lhs1, lhs2, xout,
                load_sem, own_sem, out_sem, ys_sem, yr_sem, us_sem, ur_sem, vs_sem, vr_sem):
    r = lax.axis_index("row")
    c = lax.axis_index("col")
    core = r % 2
    x = r // 8
    z = (r // 2) % 4
    pending = []

    def start(cond, build):
        if cond is None:
            build().start()
        else:
            @pl.when(cond)
            def _():
                build().start()
        pending.append((cond, build))

    def rcopy(src, dst, ssem, rsem, row, col):
        return pltpu.make_async_remote_copy(
            src_ref=src, dst_ref=dst, send_sem=ssem, recv_sem=rsem,
            device_id={"row": row, "col": col}, device_id_type=MESH)

    load_u = pltpu.make_async_copy(u_hbm, u, load_sem.at[0])
    load_v = pltpu.make_async_copy(v_hbm, v, load_sem.at[1])
    load_inv = pltpu.make_async_copy(inv_hbm, inv, load_sem.at[2])
    load_v.start()
    load_u.start()
    load_inv.start()

    barrier = pltpu.get_barrier_semaphore()
    partners = [(r + 1 - 2 * core, c)]
    for k in (1, 2, 3):
        partners.append((8 * ((x + k) % 4) + 2 * z + core, c))
        partners.append((8 * x + 2 * ((z + k) % 4) + core, c))
        partners.append((r, (c + k) % 4))
        partners.append((r + 1 - 2 * core, (c + k) % 4))
    for row, col in partners:
        pl.semaphore_signal(barrier, inc=1, device_id={"row": row, "col": col}, device_id_type=MESH)

    p1, q1, p2, q2 = order_ref[0, 0], order_ref[0, 1], order_ref[1, 0], order_ref[1, 1]
    last_row, last_col = 2 * FIXED_ROW + 1, 2 * FIXED_COL + 1
    step_row = jnp.where(p1 == last_row, 0, 1)
    step_col = jnp.where(q1 == last_col, 0, 1)
    p_other = jnp.where(p1 == last_row, p2, p1)
    q_other = jnp.where(q1 == last_col, q2, q1)
    row_other = p_other >> 1
    l_row = p_other & 1
    x_d, z_d, core_d = row_other >> 3, (row_other >> 1) & 3, row_other & 1
    l_col = q_other & 1
    if root_d == FIXED_COL:
        l_piv = jnp.int32(1)
    else:
        l_piv = jnp.where(c == root_d, l_col, 1)

    load_v.wait()
    depth = lax.broadcasted_iota(jnp.int32, (v.shape[2], v.shape[3]), 0)
    for i in range(2):
        for j in range(2):
            v[i, j] = jnp.where(depth < ranks_ref[i, j], v[i, j], jnp.zeros_like(v[i, j]))
    load_u.wait()
    for i in range(2):
        if root_d == FIXED_COL:
            vd[i] = v[i, 0]
            ud[i] = u[i, 0]
        else:
            vd[i] = v[i, l_col]
            ud[i] = u[i, l_col]

    pl.semaphore_wait(barrier, len(partners))

    routes = column_routes(root_d)
    rows_of = (128 // CHUNKS, 1024 // CHUNKS)

    def y_index(t, kappa, i, ch):
        return ((t * 2 + kappa) * 2 + i) * CHUNKS + ch

    def y_local(t, kappa, i, ch):
        n = rows_of[t]
        if t == 0:
            ref = v.at[i, 1] if kappa == 0 else vd.at[i]
        else:
            ref = u.at[i, 1] if kappa == 0 else ud.at[i]
        return ref.at[pl.ds(ch * n, n), :]

    def y_place(t, kappa, i, ch):
        n = rows_of[t]
        if t == 0:
            return colv.at[kappa, i, pl.ds(ch * n, n), :]
        return colu_hbm.at[i, pl.ds(ch * n, n), pl.ds(128 * kappa, 128)]

    def y_copy(t, kappa, i, ch, edge, from_root):
        src, dst = routes[kappa][i][edge]
        k = y_index(t, kappa, i, ch)
        place = y_place(t, kappa, i, ch)
        return rcopy(y_local(t, kappa, i, ch) if from_root else place, place,
                     ys_sem.at[3 * k + edge], yr_sem.at[k], r, dst)

    roots = (FIXED_COL, root_d)

    def y_send_roots(t):
        for ch in range(CHUNKS):
            for i in range(2):
                for kappa in range(2):
                    for edge, (src, dst) in enumerate(routes[kappa][i]):
                        if src == roots[kappa]:
                            start(c == src, functools.partial(y_copy, t, kappa, i, ch, edge, True))

    def y_forwarders(kappa, i):
        return sorted({src for src, _ in routes[kappa][i] if src != roots[kappa]})

    def y_wait(t, kappa, i, ch):
        y_copy(t, kappa, i, ch, 0, False).wait_recv()

    def y_forward(t):
        for ch in range(CHUNKS):
            for i in range(2):
                for kappa in range(2):
                    for f in y_forwarders(kappa, i):
                        @pl.when(c == f)
                        def _():
                            y_wait(t, kappa, i, ch)
                        for edge, (src, dst) in enumerate(routes[kappa][i]):
                            if src == f:
                                start(c == f, functools.partial(y_copy, t, kappa, i, ch, edge, False))

    def y_finish(t):
        for ch in range(CHUNKS):
            for i in range(2):
                for kappa in range(2):
                    for leaf in sorted(set(range(4)) - {roots[kappa]} - set(y_forwarders(kappa, i))):
                        @pl.when(c == leaf)
                        def _():
                            y_wait(t, kappa, i, ch)

    left = Kind(True, u, x, z, core, send1_u, r1_u, c2_u, s2_u, q3_u, s3_u, big_u, us_sem, ur_sem)
    right = Kind(False, v, z, x, core, send1_v, r1_v, c2_v, s2_v, q3_v, s3_v, big_v, vs_sem, vr_sem)
    kinds = (right, left)
    l_other = jnp.where(core == 0, l_piv, 1 - l_piv)
    l_own = jnp.where(core == 1, l_piv, 1 - l_piv)
    mate = r + 1 - 2 * core

    def stage1(t):
        t.send1[0] = t.src[l_row, l_other]
        start(None, lambda: rcopy(t.send1.at[0], t.r1.at[0], t.ssem.at[0], t.rsem.at[0], mate, c))

        @pl.when(r == FIXED_ROW)
        def _():
            t.send1[1] = t.src[1, l_other]
        start(r == FIXED_ROW, lambda: rcopy(t.send1.at[1], t.r1.at[1], t.ssem.at[1], t.rsem.at[1], mate, c))

    def stage2(t):
        a, b = t.a, t.b
        rcopy(t.send1.at[0], t.r1.at[0], t.ssem.at[0], t.rsem.at[0], mate, c).wait_recv()
        t.c2[0] = jnp.where(core_d == core, t.src[l_row, l_own], t.r1[0])
        for k in (1, 2, 3):
            to = (a + k) % 4
            start(None, lambda to=to, k=k: rcopy(
                t.c2.at[(0,) + t.quarter(to)], t.s2.at[a], t.ssem.at[1 + k], t.rsem.at[1 + k], t.row_of(to, b, core), c))
        t.s2[a] = t.c2[(0,) + t.quarter(a)]

        @pl.when(r == FIXED_ROW)
        def _():
            t.c2[1] = t.src[1, l_own]

        @pl.when(r == FIXED_ROW - 1)
        def _():
            rcopy(t.send1.at[1], t.r1.at[1], t.ssem.at[1], t.rsem.at[1], mate, c).wait_recv()
            t.c2[1] = t.r1[1]
        at_root = (a == 3) & (b == 3)
        for k in (1, 2, 3):
            to = (a + k) % 4
            start(at_root, lambda to=to, k=k: rcopy(
                t.c2.at[(1,) + t.quarter(to)], t.q3.at[1], t.ssem.at[4 + k], t.rsem.at[5], t.row_of(to, b, core), c))

        @pl.when(at_root)
        def _():
            t.q3[1] = t.c2[(1,) + t.quarter(3)]

    def stage3(t):
        a, b = t.a, t.b
        for k in (1, 2, 3):
            rcopy(t.c2.at[(0,) + t.quarter(0)], t.s2.at[0], t.ssem.at[1 + k], t.rsem.at[1 + k], r, c).wait_recv()
        t.q3[0] = t.s2[x_d if t.left else z_d]
        for k in (1, 2, 3):
            to = (b + k) % 4
            start(None, lambda to=to, k=k: rcopy(
                t.q3.at[(0,) + t.sub(to)], t.s3.at[b], t.ssem.at[7 + k], t.rsem.at[5 + k], t.row_of(a, to, core), c))
        t.s3[b] = t.q3[(0,) + t.sub(b)]

        @pl.when((b == 3) & (a != 3))
        def _():
            rcopy(t.q3.at[1], t.q3.at[1], t.ssem.at[5], t.rsem.at[5], r, c).wait_recv()
        for k in (1, 2, 3):
            to = (b + k) % 4
            start(b == 3, lambda to=to, k=k: rcopy(
                t.q3.at[(1,) + t.sub(to)], t.big.at[(core, 0) + t.piece(a, to)], t.ssem.at[10 + k], t.rsem.at[9],
                t.row_of(a, to, core), c))

        @pl.when(b == 3)
        def _():
            t.big[(core, 0) + t.piece(a, 3)] = t.q3[(1,) + t.sub(3)]

    def stage4(t):
        a, b = t.a, t.b
        for k in (1, 2, 3):
            rcopy(t.s3.at[0], t.s3.at[0], t.ssem.at[7 + k], t.rsem.at[5 + k], r, c).wait_recv()
        t.big[(core, 1) + t.piece(a, b)] = t.s3[z_d if t.left else x_d]

        @pl.when(b != 3)
        def _():
            rcopy(t.s3.at[0], t.s3.at[0], t.ssem.at[11], t.rsem.at[9], r, c).wait_recv()

        def cross(same):
            return jnp.where((step_row == step_col) == same, t.big[(core, 0) + t.piece(a, b)],
                             t.big[(core, 1) + t.piece(a, b)])
        spot_f = t.big.at[(1, 2) + t.piece(a, b)]
        spot_d = t.big.at[(0, 2) + t.piece(a, b)]

        @pl.when((c == FIXED_COL) & (core == 1))
        def _():
            t.big[(1, 2) + t.piece(a, b)] = cross(False)
        for col in range(3):
            start((c == FIXED_COL) & (core == 1), lambda col=col: rcopy(
                spot_f, spot_f, t.ssem.at[14 + col], t.rsem.at[10], r, col))
        if root_d == FIXED_COL:
            @pl.when((c == FIXED_COL) & (core == 0))
            def _():
                t.big[(0, 2) + t.piece(a, b)] = cross(True)
            for col in range(3):
                start((c == FIXED_COL) & (core == 0), lambda col=col: rcopy(
                    spot_d, spot_d, t.ssem.at[14 + col], t.rsem.at[10], r, col))
        else:
            @pl.when((c == root_d) & (core == 1))
            def _():
                t.s3[0] = cross(True)
            for col in range(4):
                start((c == root_d) & (core == 1), lambda col=col: rcopy(
                    t.s3.at[0], spot_d, t.ssem.at[17 + col], t.rsem.at[10], mate, col))

    def stage5(t):
        a, b = t.a, t.b
        if root_d == FIXED_COL:
            hears = c != FIXED_COL
        else:
            hears = (c != FIXED_COL) | (core == 0)

        @pl.when(hears)
        def _():
            rcopy(t.s3.at[0], t.s3.at[0], t.ssem.at[14], t.rsem.at[10], r, c).wait_recv()
        for k in (1, 2, 3):
            part = t.big.at[(core, slice(None)) + t.piece(a, b)]
            start(None, lambda k=k, part=part: rcopy(
                part, part, t.ssem.at[20 + k], t.rsem.at[10 + k], t.row_of(a, (b + k) % 4, core), c))

    def stage6(t):
        a, b = t.a, t.b
        for k in (1, 2, 3):
            part = t.big.at[(core, slice(None)) + t.piece(a, b)]
            rcopy(part, part, t.ssem.at[20 + k], t.rsem.at[10 + k], r, c).wait_recv()
        for k in (1, 2, 3):
            part = t.big.at[(core, slice(None)) + t.quarter(a)]
            start(None, lambda k=k, part=part: rcopy(
                part, part, t.ssem.at[23 + k], t.rsem.at[13 + k], t.row_of((a + k) % 4, b, core), c))

    def stage7(t):
        a, b = t.a, t.b
        for k in (1, 2, 3):
            part = t.big.at[(core, slice(None)) + t.quarter(a)]
            rcopy(part, part, t.ssem.at[23 + k], t.rsem.at[13 + k], r, c).wait_recv()
        start(None, lambda: rcopy(t.big.at[core], t.big.at[core], t.ssem.at[27], t.rsem.at[17], mate, c))

    def stage8(t):
        rcopy(t.big.at[0], t.big.at[0], t.ssem.at[27], t.rsem.at[17], r, c).wait_recv()

    y_send_roots(0)
    stage1(left)
    stage1(right)
    y_send_roots(1)
    for kappa in range(2):
        @pl.when(c == roots[kappa])
        def _():
            for i in range(2):
                colv[kappa, i] = v[i, 1] if kappa == 0 else vd[i]

    def own_copy(kappa, i):
        return pltpu.make_async_copy(
            u.at[i, 1] if kappa == 0 else ud.at[i],
            colu_hbm.at[i, :, pl.ds(128 * kappa, 128)], own_sem.at[2 * kappa + i])
    for kappa in range(2):
        for i in range(2):
            @pl.when(c == roots[kappa])
            def _():
                own_copy(kappa, i).start()

    stage2(left)
    stage2(right)
    stage3(left)
    stage3(right)
    stage4(left)
    stage4(right)
    stage5(left)
    stage5(right)
    y_forward(0)
    stage6(left)
    stage6(right)
    stage7(left)
    stage7(right)
    y_forward(1)
    stage8(left)

    load_inv.wait()
    t1, t2 = step_row, 1 - step_row

    def slot(j):
        return jnp.where(l_piv == 1, j, 1 - j)
    for n, (row_t, cross_h, solved) in enumerate(((t1, step_col, s1), (t2, 1 - step_col, s2))):
        for j in range(2):
            ucat[:, 128 * j:128 * j + 128] = big_u[slot(j), row_t]
        ucat[:, 256:384] = big_u[cross_h, 2]

        @pl.loop(0, 4)
        def _(blk):
            rows = pl.ds(pl.multiple_of(256 * blk, 256), 256)
            solved[rows, :] = jnp.dot(inv[n, rows, :], ucat[...], preferred_element_type=F32).astype(BF)

    stage8(right)
    y_finish(0)
    for n, (col_k, cross_h, solved, pm) in enumerate(
            ((step_col, 1 - step_col, s1, pm1), (1 - step_col, step_col, s2, pm2))):
        for i in range(2):
            vcat[128 * i:128 * i + 128, :] = colv[col_k, i]
        vcat[256:384, :] = big_v[cross_h, 2]
        prod = jnp.dot(vcat[...], solved[...], preferred_element_type=F32).astype(BF)
        for i in range(3):
            for j in range(3):
                pm[i, j] = prod[128 * i:128 * i + 128, 128 * j:128 * j + 128]

    one, zero = jnp.float32(1), jnp.float32(0)
    for j in range(2):
        jg = 2 * c + j
        col_live1 = jg != q1
        col_live2 = (jg != q1) & (jg != q2)
        rhs1[0:128, :] = big_v[slot(j), t1]
        rhs2[0:128, :] = big_v[slot(j), t2]
        h = (pm1[2, j].astype(F32) * jnp.where(col_live1, one, zero)).astype(BF)
        t_val = jnp.dot(h, rhs1[0:128, :], preferred_element_type=F32).astype(BF)
        rhs2[128:256, :] = t_val
        z_val = (jnp.dot(pm2[2, j], rhs2[0:128, :], preferred_element_type=F32)
                 - jnp.dot(pm2[2, 2], t_val, preferred_element_type=F32)).astype(BF)
        rhs1[128:256, :] = z_val
        for i in range(2):
            ig = 2 * r + i
            row_live1 = ig != p1
            m1 = jnp.where(row_live1 & col_live1, one, zero)
            m2 = jnp.where(row_live1 & (ig != p2) & col_live2, one, zero)
            band = slice(128 * i, 128 * i + 128)
            lhs1[band, 0:128] = (pm1[i, j].astype(F32) * -m1).astype(BF)
            lhs1[band, 128:256] = (pm1[i, 2].astype(F32) * m2).astype(BF)
            lhs2[band, 0:128] = (pm2[i, j].astype(F32) * -m2).astype(BF)
            lhs2[band, 128:256] = (pm2[i, 2].astype(F32) * m2).astype(BF)
        x1 = jnp.dot(lhs1[...], rhs1[...], preferred_element_type=F32).astype(BF)
        x2 = jnp.dot(lhs2[...], rhs2[...], preferred_element_type=F32).astype(BF)
        xf = jnp.where(step_col == 0, x1, x2)
        xd = jnp.where(step_col == 0, x2, x1)
        for i in range(2):
            xout[i, j, 0:128, :] = xf[128 * i:128 * i + 128]
            xout[i, j, 128:256, :] = xd[128 * i:128 * i + 128]
    out = pltpu.make_async_copy(xout, x_hbm, out_sem.at[0])
    out.start()
    y_finish(1)
    for kappa in range(2):
        for i in range(2):
            @pl.when(c == roots[kappa])
            def _():
                own_copy(kappa, i).wait()
    out.wait()
    for cond, build in pending:
        if cond is None:
            build().wait_send()
        else:
            @pl.when(cond)
            def _():
                build().wait_send()


def exchange(root_d, order, ranks, tile_u, tile_v, inverses):
    def bf(*shape):
        return pltpu.VMEM(shape, BF)
    n_y = 8 * CHUNKS
    dma = pltpu.SemaphoreType.DMA
    row_u = [bf(2, 1024, 128), bf(2, 1024, 128), bf(2, 1024, 128), bf(4, 256, 128), bf(2, 256, 128), bf(4, 64, 128),
             bf(2, 3, 1024, 128)]
    row_v = [bf(2, 128, 1024), bf(2, 128, 1024), bf(2, 128, 1024), bf(4, 32, 1024), bf(2, 32, 1024), bf(4, 32, 256),
             bf(2, 3, 128, 1024)]
    any_spec = pl.BlockSpec(memory_space=pl.ANY)
    smem_spec = pl.BlockSpec(memory_space=pltpu.SMEM)
    return pl.pallas_call(
        functools.partial(comm_kernel, root_d),
        out_shape=(jax.ShapeDtypeStruct((2, 1024, 256), BF), jax.ShapeDtypeStruct((2, 2, 256, 1024), BF)),
        in_specs=[smem_spec, smem_spec, any_spec, any_spec, any_spec],
        out_specs=(any_spec, any_spec),
        scratch_shapes=[
            bf(2, 2, 1024, 128), bf(2, 2, 128, 1024), bf(2, 1024, 1024), bf(2, 128, 1024), bf(2, 1024, 128),
            bf(2, 2, 128, 1024)] + row_u + row_v + [
            bf(1024, 384), bf(1024, 384), bf(1024, 384), bf(384, 1024), bf(3, 3, 128, 128), bf(3, 3, 128, 128),
            bf(256, 1024), bf(256, 1024), bf(256, 256), bf(256, 256), bf(2, 2, 256, 1024),
            dma((3,)), dma((4,)), dma((1,)), dma((3 * n_y,)), dma((n_y,)),
            dma((28,)), dma((18,)), dma((28,)), dma((18,))],
        compiler_params=pltpu.CompilerParams(
            collective_id=root_d, has_side_effects=True, vmem_limit_bytes=56 << 20),
        name="pivots_%d" % root_d,
    )(order, ranks, tile_u, tile_v, inverses)


def form_kernel(ranks_ref, u_ref, v_ref, cu_ref, x_ref, o_ref):
    i, j = pl.program_id(0), pl.program_id(1)
    right = v_ref[0, 0]
    depth = lax.broadcasted_iota(jnp.int32, right.shape, 0)
    right = jnp.where(depth < ranks_ref[i, j], right, jnp.zeros_like(right))
    o_ref[0, 0] = (jnp.dot(u_ref[0, 0], right, preferred_element_type=F32)
                   + jnp.dot(cu_ref[0], x_ref[0, 0], preferred_element_type=F32)).astype(BF)


def form(ranks, tile_u, tile_v, col_u, right):
    rows = 512
    return pl.pallas_call(
        form_kernel,
        out_shape=jax.ShapeDtypeStruct((2, 2, 1024, 1024), BF),
        grid_spec=pltpu.PrefetchScalarGridSpec(
            num_scalar_prefetch=1, grid=(2, 2, 1024 // rows),
            in_specs=[
                pl.BlockSpec((1, 1, rows, 128), lambda i, j, k, s: (i, j, k, 0)),
                pl.BlockSpec((1, 1, 128, 1024), lambda i, j, k, s: (i, j, 0, 0)),
                pl.BlockSpec((1, rows, 256), lambda i, j, k, s: (i, k, 0)),
                pl.BlockSpec((1, 1, 256, 1024), lambda i, j, k, s: (i, j, 0, 0)),
            ],
            out_specs=pl.BlockSpec((1, 1, rows, 1024), lambda i, j, k, s: (i, j, k, 0))),
        name="form_tiles",
    )(ranks, tile_u, tile_v, col_u, right)


def on_device(tile_u, tile_v, tile_ranks, inverses, panel_order):
    last_col = 2 * FIXED_COL + 1
    q_other = jnp.where(panel_order[0, 1] == last_col, panel_order[1, 1], panel_order[0, 1])
    branches = [functools.partial(exchange, root_d) for root_d in range(NY)]
    col_u, right = lax.switch(q_other // 2, branches, panel_order, tile_ranks, tile_u, tile_v, inverses)
    return form(tile_ranks, tile_u, tile_v, col_u, right)


def solution(mesh):
    placed = (P("row", "col", None, None), P("row", "col", None, None), P("row", "col"), P(), P())
    return jax.shard_map(
        on_device,
        mesh=mesh,
        in_specs=placed,
        out_specs=P("row", "col", None, None),
        check_vma=False,
    )
```

```python
import functools

import jax
import jax.numpy as jnp
from jax import lax
from jax.experimental import pallas as pl
from jax.experimental.pallas import tpu as pltpu
from jax.sharding import PartitionSpec as P

MESH = pl.DeviceIdType.MESH
BF = jnp.bfloat16
F32 = jnp.float32
NX = NZ = NY = 4
FIXED_ROW = 31
FIXED_COL = 3
CHUNKS = 2
FORM_ROWS = 256
MAIN, CROSS = 24, 31


def column_routes(root_d):
    if root_d == FIXED_COL:
        up, down = [(3, 0), (0, 1), (1, 2)], [(3, 2), (2, 1), (1, 0)]
        return [[up, down], [up, down]]
    if root_d == 1:
        fixed = [[(3, 0), (3, 2), (0, 1)], [(3, 0), (3, 2), (2, 1)]]
        other = [[(1, 2), (1, 0), (2, 3)], [(1, 2), (1, 0), (0, 3)]]
        return [fixed, other]
    if root_d == 0:
        fixed, other = [(3, 0), (3, 2), (2, 1)], [(0, 1), (0, 3), (1, 2)]
    else:
        fixed, other = [(3, 0), (3, 2), (0, 1)], [(2, 1), (2, 3), (1, 0)]
    return [[fixed, fixed], [other, other]]


class Kind:
    def __init__(self, left, src, a, b, core, send1, r1, c2, s2, q3, g3, xb, big, bx, ssem, rsem):
        self.left, self.src, self.a, self.b, self.core = left, src, a, b, core
        self.send1, self.r1, self.c2, self.s2, self.q3, self.g3, self.xb, self.big, self.bx = (
            send1, r1, c2, s2, q3, g3, xb, big, bx)
        self.ssem, self.rsem = ssem, rsem

    def row_of(self, a, b, core):
        return 8 * a + 2 * b + core if self.left else 2 * a + 8 * b + core

    def quarter(self, k):
        if self.left:
            return (pl.ds(pl.multiple_of(256 * k, 256), 256), slice(None))
        return (pl.ds(pl.multiple_of(32 * k, 32), 32), slice(None))

    def piece(self, a, b):
        if self.left:
            return (pl.ds(pl.multiple_of(256 * a + 64 * b, 64), 64), slice(None))
        return (pl.ds(pl.multiple_of(32 * a, 32), 32), pl.ds(pl.multiple_of(256 * b, 256), 256))


def comm_kernel(root_d, order_ref, ranks_ref, u_hbm, v_hbm, inv_hbm, colu_hbm, x_hbm, u_out, v_out,
                u, v, inv, vd, ud, colv,
                send1_u, r1_u, c2_u, s2_u, q3_u, g3_u, xb_u, big_u, bx_u,
                send1_v, r1_v, c2_v, s2_v, q3_v, g3_v, xb_v, big_v, bx_v,
                ucat, s1, s2, vcat, pm1, pm2, rhs1, rhs2, lhs1, lhs2, xout,
                load_sem, own_sem, out_sem, ys_sem, yr_sem, us_sem, ur_sem, vs_sem, vr_sem):
    r = lax.axis_index("row")
    c = lax.axis_index("col")
    core = r % 2
    x = r // 8
    z = (r // 2) % 4
    pending = []

    def start(cond, build):
        if cond is None:
            build().start()
        else:
            @pl.when(cond)
            def _():
                build().start()
        pending.append((cond, build))

    def rcopy(src, dst, ssem, rsem, row, col):
        return pltpu.make_async_remote_copy(
            src_ref=src, dst_ref=dst, send_sem=ssem, recv_sem=rsem,
            device_id={"row": row, "col": col}, device_id_type=MESH)

    load_u = pltpu.make_async_copy(u_hbm, u, load_sem.at[0])
    load_v = pltpu.make_async_copy(v_hbm, v, load_sem.at[1])
    load_inv = pltpu.make_async_copy(inv_hbm, inv, load_sem.at[2])
    load_v.start()
    load_u.start()

    barrier = pltpu.get_barrier_semaphore()
    partners = [(r + 1 - 2 * core, c)]
    for k in (1, 2, 3):
        partners.append((8 * ((x + k) % 4) + 2 * z + core, c))
        partners.append((8 * x + 2 * ((z + k) % 4) + core, c))
        partners.append((r, (c + k) % 4))
        partners.append((r + 1 - 2 * core, (c + k) % 4))
    for row, col in partners:
        pl.semaphore_signal(barrier, inc=1, device_id={"row": row, "col": col}, device_id_type=MESH)

    p1, q1, p2, q2 = order_ref[0, 0], order_ref[0, 1], order_ref[1, 0], order_ref[1, 1]
    last_row, last_col = 2 * FIXED_ROW + 1, 2 * FIXED_COL + 1
    step_row = jnp.where(p1 == last_row, 0, 1)
    step_col = jnp.where(q1 == last_col, 0, 1)
    p_other = jnp.where(p1 == last_row, p2, p1)
    q_other = jnp.where(q1 == last_col, q2, q1)
    row_other = p_other >> 1
    l_row = p_other & 1
    x_d, z_d, core_d = row_other >> 3, (row_other >> 1) & 3, row_other & 1
    l_col = q_other & 1
    if root_d == FIXED_COL:
        l_piv = jnp.int32(1)
    else:
        l_piv = jnp.where(c == root_d, l_col, 1)

    load_v.wait()
    depth = lax.broadcasted_iota(jnp.int32, (v.shape[2], v.shape[3]), 0)
    for i in range(2):
        for j in range(2):
            v[i, j] = jnp.where(depth < ranks_ref[i, j], v[i, j], jnp.zeros_like(v[i, j]))
    load_u.wait()
    for i in range(2):
        if root_d == FIXED_COL:
            vd[i] = v[i, 0]
            ud[i] = u[i, 0]
        else:
            vd[i] = v[i, l_col]
            ud[i] = u[i, l_col]

    load_inv.start()
    pass_u = pltpu.make_async_copy(u, u_out, load_sem.at[3])
    pass_v = pltpu.make_async_copy(v, v_out, load_sem.at[4])
    pl.semaphore_wait(barrier, len(partners))

    routes = column_routes(root_d)
    rows_of = (128 // CHUNKS, 1024 // CHUNKS)

    def y_index(t, kappa, i, ch):
        return ((t * 2 + kappa) * 2 + i) * CHUNKS + ch

    def y_local(t, kappa, i, ch):
        n = rows_of[t]
        if t == 0:
            ref = v.at[i, 1] if kappa == 0 else vd.at[i]
        else:
            ref = u.at[i, 1] if kappa == 0 else ud.at[i]
        return ref.at[pl.ds(ch * n, n), :]

    def y_place(t, kappa, i, ch):
        n = rows_of[t]
        if t == 0:
            return colv.at[kappa, i, pl.ds(ch * n, n), :]
        return colu_hbm.at[i, pl.ds(ch * n, n), pl.ds(128 * kappa, 128)]

    def y_copy(t, kappa, i, ch, edge, from_root):
        src, dst = routes[kappa][i][edge]
        k = y_index(t, kappa, i, ch)
        place = y_place(t, kappa, i, ch)
        return rcopy(y_local(t, kappa, i, ch) if from_root else place, place,
                     ys_sem.at[3 * k + edge], yr_sem.at[k], r, dst)

    roots = (FIXED_COL, root_d)

    def y_send_roots(t):
        for ch in range(CHUNKS):
            for i in range(2):
                for kappa in range(2):
                    for edge, (src, dst) in enumerate(routes[kappa][i]):
                        if src == roots[kappa]:
                            start(c == src, functools.partial(y_copy, t, kappa, i, ch, edge, True))

    def y_forwarders(kappa, i):
        return sorted({src for src, _ in routes[kappa][i] if src != roots[kappa]})

    def y_wait(t, kappa, i, ch):
        y_copy(t, kappa, i, ch, 0, False).wait_recv()

    def y_forward(t, n):
        ch, i = n // 2, n % 2
        for kappa in range(2):
            for f in y_forwarders(kappa, i):
                @pl.when(c == f)
                def _():
                    y_wait(t, kappa, i, ch)
                for edge, (src, dst) in enumerate(routes[kappa][i]):
                    if src == f:
                        start(c == f, functools.partial(y_copy, t, kappa, i, ch, edge, False))

    def y_finish(t):
        for ch in range(CHUNKS):
            for i in range(2):
                for kappa in range(2):
                    for leaf in sorted(set(range(4)) - {roots[kappa]} - set(y_forwarders(kappa, i))):
                        @pl.when(c == leaf)
                        def _():
                            y_wait(t, kappa, i, ch)

    left = Kind(True, u, x, z, core, send1_u, r1_u, c2_u, s2_u, q3_u, g3_u, xb_u, big_u, bx_u, us_sem, ur_sem)
    right = Kind(False, v, z, x, core, send1_v, r1_v, c2_v, s2_v, q3_v, g3_v, xb_v, big_v, bx_v, vs_sem, vr_sem)
    kinds = (right, left)
    l_other = jnp.where(core == 0, l_piv, 1 - l_piv)
    l_own = jnp.where(core == 1, l_piv, 1 - l_piv)
    mate = r + 1 - 2 * core

    def stage1(t):
        t.send1[0] = t.src[l_row, l_other]
        start(None, lambda: rcopy(t.send1.at[0], t.r1.at[0], t.ssem.at[0], t.rsem.at[0], mate, c))

        @pl.when(r == FIXED_ROW)
        def _():
            t.send1[1] = t.src[1, l_other]
        start(r == FIXED_ROW, lambda: rcopy(t.send1.at[1], t.r1.at[1], t.ssem.at[1], t.rsem.at[1], mate, c))

    def stage2(t):
        a, b = t.a, t.b
        rcopy(t.send1.at[0], t.r1.at[0], t.ssem.at[0], t.rsem.at[0], mate, c).wait_recv()
        t.c2[0] = jnp.where(core_d == core, t.src[l_row, l_own], t.r1[0])
        for k in (1, 2, 3):
            to = (a + k) % 4
            start(None, lambda to=to, k=k: rcopy(
                t.c2.at[(0,) + t.quarter(to)], t.s2.at[a], t.ssem.at[1 + k], t.rsem.at[1 + k], t.row_of(to, b, core), c))
        t.s2[a] = t.c2[(0,) + t.quarter(a)]

        @pl.when(r == FIXED_ROW)
        def _():
            t.c2[1] = t.src[1, l_own]

        @pl.when(r == FIXED_ROW - 1)
        def _():
            rcopy(t.send1.at[1], t.r1.at[1], t.ssem.at[1], t.rsem.at[1], mate, c).wait_recv()
            t.c2[1] = t.r1[1]
        at_root = (a == 3) & (b == 3)
        for k in (1, 2, 3):
            to = (a + k) % 4
            start(at_root, lambda to=to, k=k: rcopy(
                t.c2.at[(1,) + t.quarter(to)], t.q3.at[0], t.ssem.at[4 + k], t.rsem.at[5], t.row_of(to, b, core), c))

        @pl.when(at_root)
        def _():
            t.q3[0] = t.c2[(1,) + t.quarter(3)]

    def stage3(t):
        a, b = t.a, t.b
        for k in (1, 2, 3):
            rcopy(t.c2.at[(0,) + t.quarter(0)], t.s2.at[0], t.ssem.at[1 + k], t.rsem.at[1 + k], r, c).wait_recv()
        t.g3[b] = t.s2[x_d if t.left else z_d]
        for k in (1, 2, 3):
            start(None, lambda k=k: rcopy(
                t.g3.at[b], t.g3.at[b], t.ssem.at[7 + k], t.rsem.at[5 + k], t.row_of(a, (b + k) % 4, core), c))

        @pl.when((b == 3) & (a != 3))
        def _():
            rcopy(t.q3.at[0], t.q3.at[0], t.ssem.at[5], t.rsem.at[5], r, c).wait_recv()
        for k in (1, 2, 3):
            start(b == 3, lambda k=k: rcopy(
                t.q3.at[0], t.big.at[(core, 0) + t.quarter(a)], t.ssem.at[10 + k], t.rsem.at[9],
                t.row_of(a, (b + k) % 4, core), c))

        @pl.when(b == 3)
        def _():
            t.big[(core, 0) + t.quarter(a)] = t.q3[0]

    def spread_quarter(t, base, k, to_mate):
        a, b = t.a, t.b
        q = t.quarter((a - k) % 4 if to_mate else a)
        part = t.bx.at[(core,) + q] if base == CROSS else t.big.at[(core, slice(None)) + q]
        if to_mate:
            return rcopy(part, part, t.ssem.at[base + 3 + k], t.rsem.at[base + 3 + k], mate, c)
        return rcopy(part, part, t.ssem.at[base + k - 1], t.rsem.at[base + k - 1], t.row_of((a + k) % 4, b, core), c)

    def stage4(t):
        a, b = t.a, t.b
        for k in (1, 2, 3):
            rcopy(t.g3.at[0], t.g3.at[0], t.ssem.at[7 + k], t.rsem.at[5 + k], r, c).wait_recv()
        t.big[(core, 1) + t.quarter(a)] = t.g3[z_d if t.left else x_d]

        @pl.when(b != 3)
        def _():
            rcopy(t.q3.at[0], t.q3.at[0], t.ssem.at[11], t.rsem.at[9], r, c).wait_recv()
        for k in (1, 2, 3):
            start(None, functools.partial(spread_quarter, t, MAIN, k, False))
        start(None, functools.partial(spread_quarter, t, MAIN, 0, True))

        def cross(same):
            return jnp.where((step_row == step_col) == same, t.big[(core, 0) + t.piece(a, b)],
                             t.big[(core, 1) + t.piece(a, b)])
        spot_f = t.bx.at[(1,) + t.piece(a, b)]
        spot_d = t.bx.at[(0,) + t.piece(a, b)]

        @pl.when((c == FIXED_COL) & (core == 1))
        def _():
            t.bx[(1,) + t.piece(a, b)] = cross(False)
        for col in range(3):
            start((c == FIXED_COL) & (core == 1), lambda col=col: rcopy(
                spot_f, spot_f, t.ssem.at[14 + col], t.rsem.at[10], r, col))
        if root_d == FIXED_COL:
            @pl.when((c == FIXED_COL) & (core == 0))
            def _():
                t.bx[(0,) + t.piece(a, b)] = cross(True)
            for col in range(3):
                start((c == FIXED_COL) & (core == 0), lambda col=col: rcopy(
                    spot_d, spot_d, t.ssem.at[14 + col], t.rsem.at[10], r, col))
        else:
            @pl.when((c == root_d) & (core == 1))
            def _():
                t.xb[...] = cross(True)
            for col in range(4):
                start((c == root_d) & (core == 1), lambda col=col: rcopy(
                    t.xb, spot_d, t.ssem.at[17 + col], t.rsem.at[10], mate, col))

    def stage5(t):
        a, b = t.a, t.b
        if root_d == FIXED_COL:
            hears = c != FIXED_COL
        else:
            hears = (c != FIXED_COL) | (core == 0)

        @pl.when(hears)
        def _():
            rcopy(t.xb, t.xb, t.ssem.at[14], t.rsem.at[10], r, c).wait_recv()
        for k in (1, 2, 3):
            part = t.bx.at[(core,) + t.piece(a, b)]
            start(None, lambda k=k, part=part: rcopy(
                part, part, t.ssem.at[20 + k], t.rsem.at[10 + k], t.row_of(a, (b + k) % 4, core), c))

    def stage6(t):
        for k in (1, 2, 3):
            rcopy(t.xb, t.xb, t.ssem.at[20 + k], t.rsem.at[10 + k], r, c).wait_recv()
        for k in (1, 2, 3):
            start(None, functools.partial(spread_quarter, t, CROSS, k, False))
        start(None, functools.partial(spread_quarter, t, CROSS, 0, True))

    def stage7(t, base):
        for k in (1, 3, 2):
            spread_quarter(t, base, k, False).wait_recv()
            start(None, functools.partial(spread_quarter, t, base, k, True))

    def stage8(t, base):
        for k in range(4):
            spread_quarter(t, base, k, True).wait_recv()

    stage1(left)
    stage1(right)
    y_send_roots(0)
    y_send_roots(1)
    pass_u.start()
    pass_v.start()
    for kappa in range(2):
        @pl.when(c == roots[kappa])
        def _():
            for i in range(2):
                colv[kappa, i] = v[i, 1] if kappa == 0 else vd[i]

    def own_copy(kappa, i):
        return pltpu.make_async_copy(
            u.at[i, 1] if kappa == 0 else ud.at[i],
            colu_hbm.at[i, :, pl.ds(128 * kappa, 128)], own_sem.at[2 * kappa + i])
    for kappa in range(2):
        for i in range(2):
            @pl.when(c == roots[kappa])
            def _():
                own_copy(kappa, i).start()

    stage2(left)
    stage2(right)
    y_forward(0, 0)
    stage3(left)
    stage3(right)
    y_forward(0, 1)
    y_forward(0, 2)
    stage4(left)
    stage4(right)
    y_forward(0, 3)
    stage5(left)
    stage5(right)
    y_forward(1, 0)
    stage6(left)
    stage6(right)
    y_forward(1, 1)
    stage7(left, MAIN)
    stage7(right, MAIN)
    y_forward(1, 2)
    stage8(left, MAIN)

    load_inv.wait()
    t1, t2 = step_row, 1 - step_row

    def slot(j):
        return jnp.where(l_piv == 1, j, 1 - j)
    for n, (row_t, solved) in enumerate(((t1, s1), (t2, s2))):
        for j in range(2):
            ucat[:, 128 * j:128 * j + 128] = big_u[slot(j), row_t]

        @pl.loop(0, 4)
        def _(blk):
            rows = pl.ds(pl.multiple_of(256 * blk, 256), 256)
            solved[rows, 0:256] = jnp.dot(inv[n, rows, :], ucat[...], preferred_element_type=F32).astype(BF)

    stage7(left, CROSS)
    stage7(right, CROSS)
    y_forward(1, 3)
    stage8(left, CROSS)
    for n, (cross_h, solved) in enumerate(((step_col, s1), (1 - step_col, s2))):
        ucat[:, 0:128] = bx_u[cross_h]

        @pl.loop(0, 4)
        def _(blk):
            rows = pl.ds(pl.multiple_of(256 * blk, 256), 256)
            solved[rows, 256:384] = jnp.dot(inv[n, rows, :], ucat[:, 0:128], preferred_element_type=F32).astype(BF)

    stage8(right, MAIN)
    stage8(right, CROSS)
    y_finish(0)
    for n, (col_k, cross_h, solved, pm) in enumerate(
            ((step_col, 1 - step_col, s1, pm1), (1 - step_col, step_col, s2, pm2))):
        for i in range(2):
            vcat[128 * i:128 * i + 128, :] = colv[col_k, i]
        vcat[256:384, :] = bx_v[cross_h]
        prod = jnp.dot(vcat[...], solved[...], preferred_element_type=F32).astype(BF)
        for i in range(3):
            for j in range(3):
                pm[i, j] = prod[128 * i:128 * i + 128, 128 * j:128 * j + 128]

    def out_copy(i, j):
        return pltpu.make_async_copy(xout.at[i, j], x_hbm.at[i, j], out_sem.at[2 * i + j])

    one, zero = jnp.float32(1), jnp.float32(0)
    for j in range(2):
        jg = 2 * c + j
        col_live1 = jg != q1
        col_live2 = (jg != q1) & (jg != q2)
        rhs1[0:128, :] = big_v[slot(j), t1]
        rhs2[0:128, :] = big_v[slot(j), t2]
        h = (pm1[2, j].astype(F32) * jnp.where(col_live1, one, zero)).astype(BF)
        t_val = jnp.dot(h, rhs1[0:128, :], preferred_element_type=F32).astype(BF)
        rhs2[128:256, :] = t_val
        z_val = (jnp.dot(pm2[2, j], rhs2[0:128, :], preferred_element_type=F32)
                 - jnp.dot(pm2[2, 2], t_val, preferred_element_type=F32)).astype(BF)
        rhs1[128:256, :] = z_val
        for i in range(2):
            ig = 2 * r + i
            row_live1 = ig != p1
            m1 = jnp.where(row_live1 & col_live1, one, zero)
            m2 = jnp.where(row_live1 & (ig != p2) & col_live2, one, zero)
            band = slice(128 * i, 128 * i + 128)
            lhs1[band, 0:128] = (pm1[i, j].astype(F32) * -m1).astype(BF)
            lhs1[band, 128:256] = (pm1[i, 2].astype(F32) * m2).astype(BF)
            lhs2[band, 0:128] = (pm2[i, j].astype(F32) * -m2).astype(BF)
            lhs2[band, 128:256] = (pm2[i, 2].astype(F32) * m2).astype(BF)
        x1 = jnp.dot(lhs1[...], rhs1[...], preferred_element_type=F32).astype(BF)
        x2 = jnp.dot(lhs2[...], rhs2[...], preferred_element_type=F32).astype(BF)
        xf = jnp.where(step_col == 0, x1, x2)
        xd = jnp.where(step_col == 0, x2, x1)
        for i in range(2):
            xout[i, j, 0:128, :] = xf[128 * i:128 * i + 128]
            xout[i, j, 128:256, :] = xd[128 * i:128 * i + 128]
            out_copy(i, j).start()
    y_finish(1)
    for kappa in range(2):
        for i in range(2):
            @pl.when(c == roots[kappa])
            def _():
                own_copy(kappa, i).wait()
    for i in range(2):
        for j in range(2):
            out_copy(i, j).wait()
    pass_u.wait()
    pass_v.wait()
    for cond, build in pending:
        if cond is None:
            build().wait_send()
        else:
            @pl.when(cond)
            def _():
                build().wait_send()


def exchange(root_d, order, ranks, tile_u, tile_v, inverses):
    def bf(*shape):
        return pltpu.VMEM(shape, BF)
    n_y = 8 * CHUNKS
    dma = pltpu.SemaphoreType.DMA
    row_u = [bf(2, 1024, 128), bf(2, 1024, 128), bf(2, 1024, 128), bf(4, 256, 128), bf(1, 256, 128), bf(4, 256, 128),
             bf(64, 128), bf(2, 2, 1024, 128), bf(2, 1024, 128)]
    row_v = [bf(2, 128, 1024), bf(2, 128, 1024), bf(2, 128, 1024), bf(4, 32, 1024), bf(1, 32, 1024), bf(4, 32, 1024),
             bf(32, 256), bf(2, 2, 128, 1024), bf(2, 128, 1024)]
    any_spec = pl.BlockSpec(memory_space=pl.ANY)
    smem_spec = pl.BlockSpec(memory_space=pltpu.SMEM)
    return pl.pallas_call(
        functools.partial(comm_kernel, root_d),
        out_shape=(jax.ShapeDtypeStruct((2, 1024, 256), BF), jax.ShapeDtypeStruct((2, 2, 256, 1024), BF),
                   jax.ShapeDtypeStruct(tile_u.shape, BF), jax.ShapeDtypeStruct(tile_v.shape, BF)),
        in_specs=[smem_spec, smem_spec, any_spec, any_spec, any_spec],
        out_specs=(any_spec,) * 4,
        scratch_shapes=[
            bf(2, 2, 1024, 128), bf(2, 2, 128, 1024), bf(2, 1024, 1024), bf(2, 128, 1024), bf(2, 1024, 128),
            bf(2, 2, 128, 1024)] + row_u + row_v + [
            bf(1024, 256), bf(1024, 384), bf(1024, 384), bf(384, 1024), bf(3, 3, 128, 128), bf(3, 3, 128, 128),
            bf(256, 1024), bf(256, 1024), bf(256, 256), bf(256, 256), bf(2, 2, 256, 1024),
            dma((5,)), dma((4,)), dma((4,)), dma((3 * n_y,)), dma((n_y,)),
            dma((38,)), dma((38,)), dma((38,)), dma((38,))],
        compiler_params=pltpu.CompilerParams(
            collective_id=root_d, has_side_effects=True, vmem_limit_bytes=28 << 20),
        name="pivots_%d" % root_d,
    )(order, ranks, tile_u, tile_v, inverses)


def form_kernel(u_ref, v_ref, cu_ref, x_ref, o_hbm, tiles, sem):
    copies = []
    for i in range(2):
        for j in range(2):
            for k in range(1024 // FORM_ROWS):
                rows = pl.ds(FORM_ROWS * k, FORM_ROWS)
                tiles[i, j, rows, :] = (
                    jnp.dot(u_ref[i, j, rows, :], v_ref[i, j], preferred_element_type=F32)
                    + jnp.dot(cu_ref[i, rows, :], x_ref[i, j], preferred_element_type=F32)).astype(BF)
                copy = pltpu.make_async_copy(tiles.at[i, j, rows, :], o_hbm.at[i, j, rows, :], sem.at[len(copies)])
                copy.start()
                copies.append(copy)
    for copy in copies:
        copy.wait()


def form(tile_u, tile_v, col_u, right):
    shape = (2, 2, 1024, 1024)
    return pl.pallas_call(
        form_kernel,
        out_shape=jax.ShapeDtypeStruct(shape, BF),
        in_specs=[pl.BlockSpec(memory_space=pltpu.VMEM)] * 4,
        out_specs=pl.BlockSpec(memory_space=pl.ANY),
        scratch_shapes=[pltpu.VMEM(shape, BF), pltpu.SemaphoreType.DMA((4096 // FORM_ROWS,))],
        compiler_params=pltpu.CompilerParams(vmem_limit_bytes=14 << 20),
        name="form_tiles",
    )(tile_u, tile_v, col_u, right)


def on_device(tile_u, tile_v, tile_ranks, inverses, panel_order):
    other = panel_order[0, 1] + panel_order[1, 1] - (2 * FIXED_COL + 1)
    branches = [functools.partial(exchange, root_d) for root_d in range(NY)]
    col_u, right, left_own, right_own = lax.switch(
        lax.shift_right_logical(other, 1), branches, panel_order, tile_ranks, tile_u, tile_v, inverses)
    return form(left_own, right_own, col_u, right)


def solution(mesh):
    placed = (P("row", "col", None, None), P("row", "col", None, None), P("row", "col"), P(), P())
    return jax.shard_map(
        on_device,
        mesh=mesh,
        in_specs=placed,
        out_specs=P("row", "col", None, None),
        check_vma=False,
    )
```

```python
import functools

import jax
import jax.numpy as jnp
from jax import lax
from jax.experimental import pallas as pl
from jax.experimental.pallas import tpu as pltpu
from jax.sharding import PartitionSpec as P

MESH = pl.DeviceIdType.MESH
BF = jnp.bfloat16
F32 = jnp.float32
NY = 4
FIXED_ROW = 31
FIXED_COL = 3
CHUNKS = 2
FORM_ROWS = 256
FIX, OTH, CROSS = 24, 28, 32


def column_routes(root_d):
    if root_d == FIXED_COL:
        up, down = [(3, 0), (0, 1), (1, 2)], [(3, 2), (2, 1), (1, 0)]
        return [[up, down], [up, down]]
    if root_d == 1:
        fixed = [[(3, 0), (3, 2), (0, 1)], [(3, 0), (3, 2), (2, 1)]]
        other = [[(1, 2), (1, 0), (2, 3)], [(1, 2), (1, 0), (0, 3)]]
        return [fixed, other]
    if root_d == 0:
        fixed, other = [(3, 0), (3, 2), (2, 1)], [(0, 1), (0, 3), (1, 2)]
    else:
        fixed, other = [(3, 0), (3, 2), (0, 1)], [(2, 1), (2, 3), (1, 0)]
    return [[fixed, fixed], [other, other]]


def comm_kernel(root_d, order_ref, ranks_ref, u_hbm, v_hbm, inv_hbm, left_out, x_hbm,
                uv, v, inv, uvd, colv, send1, r1, c2, s2_u, s2_v, q3, g3_u, g3_v, xb,
                big_fu, big_fv, big_du, big_dv, bx_u, bx_v,
                ucat, solved, vcat, pm1, pm2, rhs1, rhs2, lhs1, lhs2, xout,
                load_sem, own_sem, out_sem, ys_sem, yr_sem, ssem, rsem):
    r = lax.axis_index("row")
    c = lax.axis_index("col")
    core = r % 2
    x = r // 8
    z = (r // 2) % 4
    along = ((x, z), (z, x))
    mate = r + 1 - 2 * core
    row_pending, y_pending = [], []
    s2, g3, big_f, big_d, bx = (s2_u, s2_v), (g3_u, g3_v), (big_fu, big_fv), (big_du, big_dv), (bx_u, bx_v)

    def row_of(t, a, b):
        return (2 * a + 8 * b if t else 8 * a + 2 * b) + core

    def start(cond, build, pending=row_pending):
        if cond is None:
            build().start()
        else:
            @pl.when(cond)
            def _():
                build().start()
        pending.append((cond, build))

    def flush(pending):
        for cond, build in pending:
            if cond is None:
                build().wait_send()
            else:
                @pl.when(cond)
                def _():
                    build().wait_send()

    def rcopy(src, dst, send_sem, recv_sem, row, col):
        return pltpu.make_async_remote_copy(
            src_ref=src, dst_ref=dst, send_sem=send_sem, recv_sem=recv_sem,
            device_id={"row": row, "col": col}, device_id_type=MESH)

    load_u = pltpu.make_async_copy(u_hbm, uv.at[0], load_sem.at[0])
    load_v = pltpu.make_async_copy(v_hbm, v, load_sem.at[1])
    load_inv = pltpu.make_async_copy(inv_hbm, inv, load_sem.at[2])
    load_v.start()
    load_u.start()
    pass_u = pltpu.make_async_copy(u_hbm, left_out.at[:, pl.ds(2, 2)], load_sem.at[3])

    barrier = pltpu.get_barrier_semaphore()
    partners = [(mate, c)]
    for k in (1, 2, 3):
        partners.append((8 * ((x + k) % 4) + 2 * z + core, c))
        partners.append((8 * x + 2 * ((z + k) % 4) + core, c))
        partners.append((r, (c + k) % 4))
    if root_d != FIXED_COL:
        for k in (1, 2, 3):
            partners.append((mate, (c + k) % 4))
    for row, col in partners:
        pl.semaphore_signal(barrier, inc=1, device_id={"row": row, "col": col}, device_id_type=MESH)

    p1, q1, p2, q2 = order_ref[0, 0], order_ref[0, 1], order_ref[1, 0], order_ref[1, 1]
    last_row, last_col = 2 * FIXED_ROW + 1, 2 * FIXED_COL + 1
    step_row = jnp.where(p1 == last_row, 0, 1)
    step_col = jnp.where(q1 == last_col, 0, 1)
    p_other = jnp.where(p1 == last_row, p2, p1)
    q_other = jnp.where(q1 == last_col, q2, q1)
    row_other = p_other >> 1
    l_row = p_other & 1
    x_d, z_d, core_d = row_other >> 3, (row_other >> 1) & 3, row_other & 1
    along_d = ((x_d, z_d), (z_d, x_d))
    l_col = q_other & 1
    if root_d == FIXED_COL:
        l_piv = jnp.int32(1)
    else:
        l_piv = jnp.where(c == root_d, l_col, 1)
    l_other = jnp.where(core == 0, l_piv, 1 - l_piv)
    l_own = jnp.where(core == 1, l_piv, 1 - l_piv)

    load_v.wait()
    depth = lax.broadcasted_iota(jnp.int32, v.shape[2:], 0)
    for i in range(2):
        for j in range(2):
            kept = jnp.where(depth < ranks_ref[i, j], v[i, j], jnp.zeros_like(v[i, j]))
            xout[i, j, 256:384, :] = kept
            for m in range(8):
                uv[1, i, j, 128 * m:128 * m + 128, :] = kept[:, 128 * m:128 * m + 128]
    load_u.wait()
    load_inv.start()
    pass_u.start()
    for t in range(2):
        for i in range(2):
            uvd[t, i] = uv[t, i, 0 if root_d == FIXED_COL else l_col]
        send1[0, t] = uv[t, l_row, l_other]

    @pl.when(r == FIXED_ROW)
    def _():
        for t in range(2):
            send1[1, t] = uv[t, 1, l_other]
            c2[1, t] = uv[t, 1, l_own]
    pl.semaphore_wait(barrier, len(partners))

    routes = column_routes(root_d)
    roots = (FIXED_COL, root_d)
    n_rows = 1024 // CHUNKS

    def y_forwarders(kappa, i):
        return sorted({src for src, _ in routes[kappa][i] if src != roots[kappa]})

    def y_copy(t, kappa, i, ch, edge, from_root):
        src, dst = routes[kappa][i][edge]
        k = ((t * 2 + kappa) * 2 + i) * CHUNKS + (ch or 0)
        rows = pl.ds(0, 1024) if ch is None else pl.ds(ch * n_rows, n_rows)
        place = colv.at[kappa, i, rows, :] if t else left_out.at[i, kappa, rows, :]
        here = place
        if from_root:
            here = uvd.at[t, i, rows, :] if kappa else uv.at[t, i, 1, rows, :]
        return rcopy(here, place, ys_sem.at[3 * k + edge], yr_sem.at[k], r, dst)

    def y_edges(kappa, i):
        out = []
        for edge, (src, dst) in enumerate(routes[kappa][i]):
            from_root = src == roots[kappa]
            out.append((edge, src, dst, from_root, not from_root or dst in y_forwarders(kappa, i)))
        return out

    def y_send_roots(t, *chunks):
        for n in chunks:
            ch, i = n // 2, n % 2
            for kappa in range(2):
                for edge, src, dst, from_root, chunked in y_edges(kappa, i):
                    if from_root and (chunked or ch == 0):
                        start(c == src, functools.partial(
                            y_copy, t, kappa, i, ch if chunked else None, edge, True), y_pending)

    def y_forward(t, n):
        ch, i = n // 2, n % 2
        for kappa in range(2):
            for f in y_forwarders(kappa, i):
                @pl.when(c == f)
                def _():
                    y_copy(t, kappa, i, ch, 0, False).wait_recv()
                for edge, src, dst, from_root, chunked in y_edges(kappa, i):
                    if src == f:
                        start(c == f, functools.partial(y_copy, t, kappa, i, ch, edge, False), y_pending)

    def y_finish(t):
        for i in range(2):
            for kappa in range(2):
                for edge, src, dst, from_root, chunked in y_edges(kappa, i):
                    if dst not in y_forwarders(kappa, i):
                        @pl.when(c == dst)
                        def _():
                            for ch in range(CHUNKS) if chunked else (None,):
                                y_copy(t, kappa, i, ch, edge, False).wait_recv()

    def quarter(k):
        return (pl.ds(pl.multiple_of(256 * k, 256), 256), slice(None))

    def first_axis(t, tile, k, dst, recv):
        a, b = along[t]
        to = (a + k) % 4
        return rcopy(c2.at[(tile, t) + quarter(to)], dst, ssem.at[t, 2 + 3 * tile + k], recv, row_of(t, to, b), c)

    def stage1():
        start(r == FIXED_ROW, lambda: rcopy(send1.at[1], r1.at[1], ssem.at[0, 1], rsem.at[0, 1], mate, c))
        start(None, lambda: rcopy(send1.at[0], r1.at[0], ssem.at[0, 0], rsem.at[0, 0], mate, c))

    def stage2_fixed():
        @pl.when(r == FIXED_ROW - 1)
        def _():
            rcopy(send1.at[1], r1.at[1], ssem.at[0, 1], rsem.at[0, 1], mate, c).wait_recv()
            c2[1] = r1[1]
        at_root = (x == 3) & (z == 3)
        for k in (1, 2, 3):
            for t in range(2):
                start(at_root, lambda k=k, t=t: first_axis(t, 1, k, q3.at[t], rsem.at[t, 2]))

        @pl.when(at_root)
        def _():
            for t in range(2):
                q3[t] = c2[(1, t) + quarter(3)]

    def stage2():
        rcopy(send1.at[0], r1.at[0], ssem.at[0, 0], rsem.at[0, 0], mate, c).wait_recv()
        for t in range(2):
            c2[0, t] = jnp.where(core_d == core, uv[t, l_row, l_own], r1[0, t])
        for k in (1, 2, 3):
            for t in range(2):
                start(None, lambda k=k, t=t: first_axis(t, 0, k, s2[t].at[along[t][0]], rsem.at[t, 2 + k]))
        for t in range(2):
            s2[t][along[t][0]] = c2[(0, t) + quarter(along[t][0])]

    def stage3_fixed(t):
        a, b = along[t]

        @pl.when((b == 3) & (a != 3))
        def _():
            rcopy(q3.at[t], q3.at[t], ssem.at[t, 5], rsem.at[t, 2], r, c).wait_recv()
        for k in (1, 2, 3):
            start(b == 3, lambda k=k: rcopy(
                q3.at[t], big_f[t].at[(core,) + quarter(a)], ssem.at[t, 8 + k], rsem.at[t, 6],
                row_of(t, a, (b + k) % 4), c))

        @pl.when(b == 3)
        def _():
            big_f[t][(core,) + quarter(a)] = q3[t]

    def stage3(t):
        a, b = along[t]
        for k in (1, 2, 3):
            first_axis(t, 0, k, s2[t].at[0], rsem.at[t, 2 + k]).wait_recv()
        g3[t][b] = s2[t][along_d[t][0]]
        for k in (1, 2, 3):
            start(None, lambda k=k: rcopy(
                g3[t].at[b], g3[t].at[b], ssem.at[t, 11 + k], rsem.at[t, 6 + k], row_of(t, a, (b + k) % 4), c))

    buffers = {FIX: big_f, OTH: big_d, CROSS: bx}

    def to_axis(t, base, k):
        a, b = along[t]
        part = buffers[base][t].at[(core,) + quarter(a)]
        return rcopy(part, part, ssem.at[t, base + k], rsem.at[t, base + k], row_of(t, (a + k) % 4, b), c)

    def to_mate(t, base):
        part = buffers[base][t].at[core]
        return rcopy(part, part, ssem.at[t, base], rsem.at[t, base], mate, c)

    def spread(t, base):
        for k in (1, 2, 3):
            start(None, functools.partial(to_axis, t, base, k))

    def stage4_fixed(t):
        @pl.when(along[t][1] != 3)
        def _():
            rcopy(q3.at[t], q3.at[t], ssem.at[t, 9], rsem.at[t, 6], r, c).wait_recv()
        spread(t, FIX)

    def stage4(t):
        a, b = along[t]
        for k in (1, 2, 3):
            rcopy(g3[t].at[0], g3[t].at[0], ssem.at[t, 11 + k], rsem.at[t, 6 + k], r, c).wait_recv()
        mine = (core,) + quarter(a)
        big_d[t][mine] = g3[t][along_d[t][1]]

        def cross(same):
            return jnp.where((step_row == step_col) == same, big_f[t][mine], big_d[t][mine])
        spot_f = bx[t].at[(1,) + quarter(a)]

        @pl.when((c == FIXED_COL) & (core == 1))
        def _():
            bx[t][(1,) + quarter(a)] = cross(False)
        for col in range(3):
            start((c == FIXED_COL) & (core == 1), lambda col=col: rcopy(
                spot_f, spot_f, ssem.at[t, 15 + col], rsem.at[t, 10], r, col))
        spot_d = bx[t].at[(0,) + quarter(a)]
        if root_d == FIXED_COL:
            @pl.when((c == FIXED_COL) & (core == 0))
            def _():
                bx[t][(0,) + quarter(a)] = cross(True)
            for col in range(3):
                start((c == FIXED_COL) & (core == 0), lambda col=col: rcopy(
                    spot_d, spot_d, ssem.at[t, 18 + col], rsem.at[t, 10], r, col))
        else:
            @pl.when((c == root_d) & (core == 1))
            def _():
                xb[t] = cross(True)
            for col in range(4):
                start((c == root_d) & (core == 1), lambda col=col: rcopy(
                    xb.at[t], spot_d, ssem.at[t, 18 + col], rsem.at[t, 10], mate, col))
        spread(t, OTH)

    def stage5(t):
        if root_d == FIXED_COL:
            hears = c != FIXED_COL
        else:
            hears = (c != FIXED_COL) | (core == 0)

        @pl.when(hears)
        def _():
            rcopy(xb.at[t], xb.at[t], ssem.at[t, 15], rsem.at[t, 10], r, c).wait_recv()
        spread(t, CROSS)

    def stage7(t, base):
        for k in (1, 2, 3):
            to_axis(t, base, k).wait_recv()
        start(None, functools.partial(to_mate, t, base))

    def stage8(t, base):
        to_mate(t, base).wait_recv()

    def both(stage, *more):
        for t in range(2):
            stage(t, *more)

    def slot(j):
        return jnp.where(l_piv == 1, j, 1 - j)

    t1, t2 = step_row, 1 - step_row

    def solve_main(row_t, step, big):
        for j in range(2):
            ucat[:, 128 * j:128 * j + 128] = big[slot(j)]

        @pl.loop(0, 4)
        def _(blk):
            rows = pl.ds(pl.multiple_of(256 * blk, 256), 256)
            solved[row_t, rows, 0:256] = jnp.dot(inv[step, rows, :], ucat[...], preferred_element_type=F32).astype(BF)

    def solve_cross(row_t, step, col_h):
        ucat[:, 0:128] = bx_u[col_h]

        @pl.loop(0, 4)
        def _(blk):
            rows = pl.ds(pl.multiple_of(256 * blk, 256), 256)
            solved[row_t, rows, 256:384] = jnp.dot(
                inv[step, rows, :], ucat[:, 0:128], preferred_element_type=F32).astype(BF)

    def forward(t, *chunks):
        for n in chunks:
            y_forward(t, n)

    def unfold(ref, rows, tile):
        for m in range(8):
            ref[rows, 128 * m:128 * m + 128] = tile[128 * m:128 * m + 128, :]

    stage1()
    stage2_fixed()
    y_send_roots(1, 0, 1, 2, 3)
    stage2()
    for kappa in range(2):
        @pl.when(c == roots[kappa])
        def _():
            for i in range(2):
                colv[kappa, i] = uvd[1, i] if kappa else uv[1, i, 1]

    def own_copy(kappa, i):
        return pltpu.make_async_copy(
            uvd.at[0, i] if kappa else uv.at[0, i, 1],
            left_out.at[i, kappa], own_sem.at[2 * kappa + i])
    for kappa in range(2):
        for i in range(2):
            @pl.when(c == roots[kappa])
            def _():
                own_copy(kappa, i).start()
    forward(1, 0)
    both(stage3_fixed)
    both(stage3)
    y_send_roots(0, 0)
    forward(1, 1)
    both(stage4_fixed)
    forward(1, 2)
    both(stage4)
    y_send_roots(0, 1, 2, 3)
    forward(1, 3)
    both(stage7, FIX)
    both(stage5)
    forward(0, 0)
    load_inv.wait()
    stage8(0, FIX)
    solve_main(0, t1, big_fu)
    both(stage7, OTH)
    forward(0, 1)
    both(stage7, CROSS)
    stage8(0, OTH)
    solve_main(1, t2, big_du)
    forward(0, 2)
    stage8(0, CROSS)
    same = step_row == step_col
    solve_cross(0, t1, jnp.where(same, 0, 1))
    solve_cross(1, t2, jnp.where(same, 1, 0))
    forward(0, 3)
    stage8(1, FIX)
    stage8(1, OTH)
    stage8(1, CROSS)
    y_finish(1)
    for col_k, cross_h, row_t, pm in ((step_col, 1 - step_col, t1, pm1), (1 - step_col, step_col, t2, pm2)):
        for i in range(2):
            unfold(vcat, slice(128 * i, 128 * i + 128), colv[col_k, i])
        unfold(vcat, slice(256, 384), bx_v[cross_h])
        prod = jnp.dot(vcat[...], solved[row_t], preferred_element_type=F32).astype(BF)
        for i in range(3):
            for j in range(3):
                pm[i, j] = prod[128 * i:128 * i + 128, 128 * j:128 * j + 128]

    def out_copy(i, j):
        return pltpu.make_async_copy(xout.at[i, j], x_hbm.at[i, j], out_sem.at[2 * i + j])

    one, zero = jnp.float32(1), jnp.float32(0)
    for j in range(2):
        jg = 2 * c + j
        col_live1 = jg != q1
        col_live2 = (jg != q1) & (jg != q2)
        right_f, right_d = big_fv[slot(j)], big_dv[slot(j)]
        unfold(rhs1, slice(0, 128), jnp.where(step_row == 0, right_f, right_d))
        unfold(rhs2, slice(0, 128), jnp.where(step_row == 0, right_d, right_f))
        h = (pm1[2, j].astype(F32) * jnp.where(col_live1, one, zero)).astype(BF)
        t_val = jnp.dot(h, rhs1[0:128, :], preferred_element_type=F32).astype(BF)
        rhs2[128:256, :] = t_val
        z_val = (jnp.dot(pm2[2, j], rhs2[0:128, :], preferred_element_type=F32)
                 - jnp.dot(pm2[2, 2], t_val, preferred_element_type=F32)).astype(BF)
        rhs1[128:256, :] = z_val
        for i in range(2):
            ig = 2 * r + i
            row_live1 = ig != p1
            m1 = jnp.where(row_live1 & col_live1, one, zero)
            m2 = jnp.where(row_live1 & (ig != p2) & col_live2, one, zero)
            band = slice(128 * i, 128 * i + 128)
            lhs1[band, 0:128] = (pm1[i, j].astype(F32) * -m1).astype(BF)
            lhs1[band, 128:256] = (pm1[i, 2].astype(F32) * m2).astype(BF)
            lhs2[band, 0:128] = (pm2[i, j].astype(F32) * -m2).astype(BF)
            lhs2[band, 128:256] = (pm2[i, 2].astype(F32) * m2).astype(BF)
        x1 = jnp.dot(lhs1[...], rhs1[...], preferred_element_type=F32).astype(BF)
        x2 = jnp.dot(lhs2[...], rhs2[...], preferred_element_type=F32).astype(BF)
        xf = jnp.where(step_col == 0, x1, x2)
        xd = jnp.where(step_col == 0, x2, x1)
        for i in range(2):
            xout[i, j, 0:128, :] = xf[128 * i:128 * i + 128]
            xout[i, j, 128:256, :] = xd[128 * i:128 * i + 128]
            out_copy(i, j).start()
    flush(row_pending)
    y_finish(0)
    for kappa in range(2):
        for i in range(2):
            @pl.when(c == roots[kappa])
            def _():
                own_copy(kappa, i).wait()
    for i in range(2):
        for j in range(2):
            out_copy(i, j).wait()
    pass_u.wait()
    flush(y_pending)


def exchange(root_d, order, ranks, tile_u, tile_v, inverses):
    def bf(*shape):
        return pltpu.VMEM(shape, BF)
    n_y = 8 * CHUNKS
    dma = pltpu.SemaphoreType.DMA
    any_spec = pl.BlockSpec(memory_space=pl.ANY)
    smem_spec = pl.BlockSpec(memory_space=pltpu.SMEM)
    return pl.pallas_call(
        functools.partial(comm_kernel, root_d),
        out_shape=(jax.ShapeDtypeStruct((2, 4, 1024, 128), BF), jax.ShapeDtypeStruct((2, 2, 384, 1024), BF)),
        in_specs=[smem_spec, smem_spec, any_spec, any_spec, any_spec],
        out_specs=(any_spec,) * 2,
        scratch_shapes=[
            bf(2, 2, 2, 1024, 128), bf(2, 2, 128, 1024), bf(2, 1024, 1024), bf(2, 2, 1024, 128), bf(2, 2, 1024, 128),
            bf(2, 2, 1024, 128), bf(2, 2, 1024, 128), bf(2, 2, 1024, 128), bf(4, 256, 128), bf(4, 256, 128),
            bf(2, 256, 128), bf(4, 256, 128), bf(4, 256, 128), bf(2, 256, 128)] + [bf(2, 1024, 128)] * 6 + [
            bf(1024, 256), bf(2, 1024, 384), bf(384, 1024), bf(3, 3, 128, 128), bf(3, 3, 128, 128),
            bf(256, 1024), bf(256, 1024), bf(256, 256), bf(256, 256), bf(2, 2, 384, 1024),
            dma((4,)), dma((4,)), dma((4,)), dma((3 * n_y,)), dma((n_y,)), dma((2, 36)), dma((2, 36))],
        compiler_params=pltpu.CompilerParams(
            collective_id=root_d, has_side_effects=True, vmem_limit_bytes=27 << 20),
        name="pivots_%d" % root_d,
    )(order, ranks, tile_u, tile_v, inverses)


def form_kernel(left_ref, right_ref, o_hbm, tiles, sem):
    copies = []
    for i in range(2):
        for j in range(2):
            for k in range(1024 // FORM_ROWS):
                rows = pl.ds(FORM_ROWS * k, FORM_ROWS)
                left = jnp.concatenate([left_ref[i, 0, rows, :], left_ref[i, 1, rows, :], left_ref[i, 2 + j, rows, :]], 1)
                tiles[i, j, rows, :] = jnp.dot(left, right_ref[i, j], preferred_element_type=F32).astype(BF)
                copy = pltpu.make_async_copy(tiles.at[i, j, rows, :], o_hbm.at[i, j, rows, :], sem.at[len(copies)])
                copy.start()
                copies.append(copy)
    for copy in copies:
        copy.wait()


def form(left, right):
    shape = (2, 2, 1024, 1024)
    return pl.pallas_call(
        form_kernel,
        out_shape=jax.ShapeDtypeStruct(shape, BF),
        in_specs=[pl.BlockSpec(memory_space=pltpu.VMEM)] * 2,
        out_specs=pl.BlockSpec(memory_space=pl.ANY),
        scratch_shapes=[pltpu.VMEM(shape, BF), pltpu.SemaphoreType.DMA((4096 // FORM_ROWS,))],
        compiler_params=pltpu.CompilerParams(vmem_limit_bytes=14 << 20),
        name="form_tiles",
    )(left, right)


def on_device(tile_u, tile_v, tile_ranks, inverses, panel_order):
    other = panel_order[0, 1] + panel_order[1, 1] - (2 * FIXED_COL + 1)
    branches = [functools.partial(exchange, root_d) for root_d in range(NY)]
    left, right = lax.switch(
        lax.shift_right_logical(other, 1), branches, panel_order, tile_ranks, tile_u, tile_v, inverses)
    return form(left, right)


def solution(mesh):
    placed = (P("row", "col", None, None), P("row", "col", None, None), P("row", "col"), P(), P())
    return jax.shard_map(
        on_device,
        mesh=mesh,
        in_specs=placed,
        out_specs=P("row", "col", None, None),
        check_vma=False,
    )
```

```python
import functools

import jax
import jax.numpy as jnp
from jax import lax
from jax.experimental import pallas as pl
from jax.experimental.pallas import tpu as pltpu
from jax.sharding import PartitionSpec as P

MESH = pl.DeviceIdType.MESH
BF = jnp.bfloat16
F32 = jnp.float32
NY = 4
FIXED_ROW = 31
FIXED_COL = 3
BOUNDS = (0, 512, 896, 1024)
CHUNKS = len(BOUNDS) - 1
FORM_ROWS = 256
FIX, OTH, CROSS = 24, 28, 32


def column_routes(root_d):
    if root_d == FIXED_COL:
        up, down = [(3, 0), (0, 1), (1, 2)], [(3, 2), (2, 1), (1, 0)]
        return [[up, down], [up, down]]
    if root_d == 1:
        fixed = [[(3, 0), (3, 2), (0, 1)], [(3, 0), (3, 2), (2, 1)]]
        other = [[(1, 2), (1, 0), (2, 3)], [(1, 2), (1, 0), (0, 3)]]
        return [fixed, other]
    if root_d == 0:
        fixed, other = [(3, 0), (3, 2), (2, 1)], [(0, 1), (0, 3), (1, 2)]
    else:
        fixed, other = [(3, 0), (3, 2), (0, 1)], [(2, 1), (2, 3), (1, 0)]
    return [[fixed, fixed], [other, other]]


def comm_kernel(root_d, order_ref, ranks_ref, u_hbm, v_hbm, inv_hbm, left_out, x_hbm,
                uv, v, inv, uvd, colv, send1, r1, c2, s2_u, s2_v, q3, g3_u, g3_v, xb,
                big_fu, big_fv, big_du, big_dv, bx_u, bx_v,
                ucat, solved, vcat, pm1, pm2, rhs1, rhs2, lhs1, lhs2, xout,
                load_sem, own_sem, out_sem, ys_sem, yr_sem, ssem, rsem):
    r = lax.axis_index("row")
    c = lax.axis_index("col")
    core = r % 2
    x = r // 8
    z = (r // 2) % 4
    along = ((x, z), (z, x))
    mate = r + 1 - 2 * core
    row_pending, y_pending = [], []
    s2, g3, big_f, big_d, bx = (s2_u, s2_v), (g3_u, g3_v), (big_fu, big_fv), (big_du, big_dv), (bx_u, bx_v)

    def row_of(t, a, b):
        return (2 * a + 8 * b if t else 8 * a + 2 * b) + core

    def start(cond, build, pending=row_pending):
        if cond is None:
            build().start()
        else:
            @pl.when(cond)
            def _():
                build().start()
        pending.append((cond, build))

    def flush(pending):
        for cond, build in pending:
            if cond is None:
                build().wait_send()
            else:
                @pl.when(cond)
                def _():
                    build().wait_send()

    def rcopy(src, dst, send_sem, recv_sem, row, col):
        return pltpu.make_async_remote_copy(
            src_ref=src, dst_ref=dst, send_sem=send_sem, recv_sem=recv_sem,
            device_id={"row": row, "col": col}, device_id_type=MESH)

    load_u = pltpu.make_async_copy(u_hbm, uv.at[0], load_sem.at[0])
    load_v = pltpu.make_async_copy(v_hbm, v, load_sem.at[1])
    load_inv = pltpu.make_async_copy(inv_hbm, inv, load_sem.at[2])
    load_v.start()
    load_u.start()

    barrier = pltpu.get_barrier_semaphore()
    partners = [(mate, c)]
    for k in (1, 2, 3):
        partners.append((8 * ((x + k) % 4) + 2 * z + core, c))
        partners.append((8 * x + 2 * ((z + k) % 4) + core, c))
        partners.append((r, (c + k) % 4))
    if root_d != FIXED_COL:
        for k in (1, 2, 3):
            partners.append((mate, (c + k) % 4))
    for row, col in partners:
        pl.semaphore_signal(barrier, inc=1, device_id={"row": row, "col": col}, device_id_type=MESH)

    p1, q1, p2, q2 = order_ref[0, 0], order_ref[0, 1], order_ref[1, 0], order_ref[1, 1]
    last_row, last_col = 2 * FIXED_ROW + 1, 2 * FIXED_COL + 1
    step_row = jnp.where(p1 == last_row, 0, 1)
    step_col = jnp.where(q1 == last_col, 0, 1)
    p_other = jnp.where(p1 == last_row, p2, p1)
    q_other = jnp.where(q1 == last_col, q2, q1)
    row_other = p_other >> 1
    l_row = p_other & 1
    x_d, z_d, core_d = row_other >> 3, (row_other >> 1) & 3, row_other & 1
    along_d = ((x_d, z_d), (z_d, x_d))
    l_col = q_other & 1
    if root_d == FIXED_COL:
        l_piv = jnp.int32(1)
    else:
        l_piv = jnp.where(c == root_d, l_col, 1)
    l_other = jnp.where(core == 0, l_piv, 1 - l_piv)
    l_own = jnp.where(core == 1, l_piv, 1 - l_piv)

    load_v.wait()
    depth = lax.broadcasted_iota(jnp.int32, v.shape[2:], 0)
    for i in range(2):
        for j in range(2):
            kept = jnp.where(depth < ranks_ref[i, j], v[i, j], jnp.zeros_like(v[i, j]))
            for m in range(8):
                uv[1, i, j, 128 * m:128 * m + 128, :] = kept[:, 128 * m:128 * m + 128]
    load_u.wait()
    load_inv.start()
    for t in range(2):
        for i in range(2):
            uvd[t, i] = uv[t, i, 0 if root_d == FIXED_COL else l_col]
        send1[0, t] = uv[t, l_row, l_other]

    @pl.when(r == FIXED_ROW)
    def _():
        for t in range(2):
            send1[1, t] = uv[t, 1, l_other]
            c2[1, t] = uv[t, 1, l_own]
    pl.semaphore_wait(barrier, len(partners))

    routes = column_routes(root_d)
    roots = (FIXED_COL, root_d)

    def y_forwarders(kappa, i):
        return sorted({src for src, _ in routes[kappa][i] if src != roots[kappa]})

    def y_copy(t, kappa, i, ch, edge, from_root):
        src, dst = routes[kappa][i][edge]
        k = ((t * 2 + kappa) * 2 + i) * CHUNKS + (ch or 0)
        rows = pl.ds(0, 1024) if ch is None else pl.ds(BOUNDS[ch], BOUNDS[ch + 1] - BOUNDS[ch])
        place = colv.at[kappa, i, rows, :] if t else left_out.at[i, kappa, rows, :]
        here = place
        if from_root:
            here = uvd.at[t, i, rows, :] if kappa else uv.at[t, i, 1, rows, :]
        return rcopy(here, place, ys_sem.at[3 * k + edge], yr_sem.at[k], r, dst)

    def y_edges(kappa, i):
        out = []
        for edge, (src, dst) in enumerate(routes[kappa][i]):
            from_root = src == roots[kappa]
            out.append((edge, src, dst, from_root, not from_root or dst in y_forwarders(kappa, i)))
        return out

    def y_send_roots(t, *chunks):
        for n in chunks:
            ch, i = n // 2, n % 2
            for kappa in range(2):
                for edge, src, dst, from_root, chunked in y_edges(kappa, i):
                    if from_root and (chunked or ch == 0):
                        start(c == src, functools.partial(
                            y_copy, t, kappa, i, ch if chunked else None, edge, True), y_pending)

    def y_forward(t, n):
        ch, i = n // 2, n % 2
        for kappa in range(2):
            for f in y_forwarders(kappa, i):
                @pl.when(c == f)
                def _():
                    y_copy(t, kappa, i, ch, 0, False).wait_recv()
                for edge, src, dst, from_root, chunked in y_edges(kappa, i):
                    if src == f:
                        start(c == f, functools.partial(y_copy, t, kappa, i, ch, edge, False), y_pending)

    def y_finish(t):
        for i in range(2):
            for kappa in range(2):
                for edge, src, dst, from_root, chunked in y_edges(kappa, i):
                    if dst not in y_forwarders(kappa, i):
                        @pl.when(c == dst)
                        def _():
                            for ch in range(CHUNKS) if chunked else (None,):
                                y_copy(t, kappa, i, ch, edge, False).wait_recv()

    def quarter(k):
        return (pl.ds(pl.multiple_of(256 * k, 256), 256), slice(None))

    def first_axis(t, tile, k, dst, recv):
        a, b = along[t]
        to = (a + k) % 4
        return rcopy(c2.at[(tile, t) + quarter(to)], dst, ssem.at[t, 2 + 3 * tile + k], recv, row_of(t, to, b), c)

    def stage1():
        start(r == FIXED_ROW, lambda: rcopy(send1.at[1], r1.at[1], ssem.at[0, 1], rsem.at[0, 1], mate, c))
        start(None, lambda: rcopy(send1.at[0], r1.at[0], ssem.at[0, 0], rsem.at[0, 0], mate, c))

    def stage2_fixed():
        @pl.when(r == FIXED_ROW - 1)
        def _():
            rcopy(send1.at[1], r1.at[1], ssem.at[0, 1], rsem.at[0, 1], mate, c).wait_recv()
            c2[1] = r1[1]
        at_root = (x == 3) & (z == 3)
        for k in (1, 2, 3):
            for t in range(2):
                start(at_root, lambda k=k, t=t: first_axis(t, 1, k, q3.at[t], rsem.at[t, 2]))

        @pl.when(at_root)
        def _():
            for t in range(2):
                q3[t] = c2[(1, t) + quarter(3)]

    def stage2():
        rcopy(send1.at[0], r1.at[0], ssem.at[0, 0], rsem.at[0, 0], mate, c).wait_recv()
        for t in range(2):
            c2[0, t] = jnp.where(core_d == core, uv[t, l_row, l_own], r1[0, t])
        for k in (1, 2, 3):
            for t in range(2):
                start(None, lambda k=k, t=t: first_axis(t, 0, k, s2[t].at[along[t][0]], rsem.at[t, 2 + k]))
        for t in range(2):
            s2[t][along[t][0]] = c2[(0, t) + quarter(along[t][0])]

    def stage3_fixed(t):
        a, b = along[t]

        @pl.when((b == 3) & (a != 3))
        def _():
            rcopy(q3.at[t], q3.at[t], ssem.at[t, 5], rsem.at[t, 2], r, c).wait_recv()
        for k in (1, 2, 3):
            start(b == 3, lambda k=k: rcopy(
                q3.at[t], big_f[t].at[(core,) + quarter(a)], ssem.at[t, 8 + k], rsem.at[t, 6],
                row_of(t, a, (b + k) % 4), c))

        @pl.when(b == 3)
        def _():
            big_f[t][(core,) + quarter(a)] = q3[t]

    def stage3(t):
        a, b = along[t]
        for k in (1, 2, 3):
            first_axis(t, 0, k, s2[t].at[0], rsem.at[t, 2 + k]).wait_recv()
        g3[t][b] = s2[t][along_d[t][0]]
        for k in (1, 2, 3):
            start(None, lambda k=k: rcopy(
                g3[t].at[b], g3[t].at[b], ssem.at[t, 11 + k], rsem.at[t, 6 + k], row_of(t, a, (b + k) % 4), c))

    buffers = {FIX: big_f, OTH: big_d, CROSS: bx}

    def to_axis(t, base, k):
        a, b = along[t]
        part = buffers[base][t].at[(core,) + quarter(a)]
        return rcopy(part, part, ssem.at[t, base + k], rsem.at[t, base + k], row_of(t, (a + k) % 4, b), c)

    def to_mate(t, base):
        part = buffers[base][t].at[core]
        return rcopy(part, part, ssem.at[t, base], rsem.at[t, base], mate, c)

    def spread(t, base):
        for k in (1, 2, 3):
            start(None, functools.partial(to_axis, t, base, k))

    def stage4_fixed(t):
        @pl.when(along[t][1] != 3)
        def _():
            rcopy(q3.at[t], q3.at[t], ssem.at[t, 9], rsem.at[t, 6], r, c).wait_recv()
        spread(t, FIX)

    def stage4(t):
        a, b = along[t]
        for k in (1, 2, 3):
            rcopy(g3[t].at[0], g3[t].at[0], ssem.at[t, 11 + k], rsem.at[t, 6 + k], r, c).wait_recv()
        mine = (core,) + quarter(a)
        big_d[t][mine] = g3[t][along_d[t][1]]

        def cross(same):
            return jnp.where((step_row == step_col) == same, big_f[t][mine], big_d[t][mine])
        spot_f = bx[t].at[(1,) + quarter(a)]

        @pl.when((c == FIXED_COL) & (core == 1))
        def _():
            bx[t][(1,) + quarter(a)] = cross(False)
        for col in range(3):
            start((c == FIXED_COL) & (core == 1), lambda col=col: rcopy(
                spot_f, spot_f, ssem.at[t, 15 + col], rsem.at[t, 10], r, col))
        spot_d = bx[t].at[(0,) + quarter(a)]
        if root_d == FIXED_COL:
            @pl.when((c == FIXED_COL) & (core == 0))
            def _():
                bx[t][(0,) + quarter(a)] = cross(True)
            for col in range(3):
                start((c == FIXED_COL) & (core == 0), lambda col=col: rcopy(
                    spot_d, spot_d, ssem.at[t, 18 + col], rsem.at[t, 10], r, col))
        else:
            @pl.when((c == root_d) & (core == 1))
            def _():
                xb[t] = cross(True)
            for col in range(4):
                start((c == root_d) & (core == 1), lambda col=col: rcopy(
                    xb.at[t], spot_d, ssem.at[t, 18 + col], rsem.at[t, 10], mate, col))
        spread(t, OTH)

    def stage5(t):
        if root_d == FIXED_COL:
            hears = c != FIXED_COL
        else:
            hears = (c != FIXED_COL) | (core == 0)

        @pl.when(hears)
        def _():
            rcopy(xb.at[t], xb.at[t], ssem.at[t, 15], rsem.at[t, 10], r, c).wait_recv()
        spread(t, CROSS)

    def stage7(t, base):
        for k in (1, 2, 3):
            to_axis(t, base, k).wait_recv()
        start(None, functools.partial(to_mate, t, base))

    def stage8(t, base):
        to_mate(t, base).wait_recv()

    def both(stage, *more):
        for t in range(2):
            stage(t, *more)

    def slot(j):
        return jnp.where(l_piv == 1, j, 1 - j)

    t1, t2 = step_row, 1 - step_row

    def solve_main(row_t, step, big):
        for j in range(2):
            ucat[:, 128 * j:128 * j + 128] = big[slot(j)]

        @pl.loop(0, 4)
        def _(blk):
            rows = pl.ds(pl.multiple_of(256 * blk, 256), 256)
            solved[row_t, rows, 0:256] = jnp.dot(inv[step, rows, :], ucat[...], preferred_element_type=F32).astype(BF)

    def solve_cross(row_t, step, col_h):
        ucat[:, 0:128] = bx_u[col_h]

        @pl.loop(0, 4)
        def _(blk):
            rows = pl.ds(pl.multiple_of(256 * blk, 256), 256)
            solved[row_t, rows, 256:384] = jnp.dot(
                inv[step, rows, :], ucat[:, 0:128], preferred_element_type=F32).astype(BF)

    def forward(t, *chunks):
        for n in chunks:
            y_forward(t, n)

    def unfold(ref, rows, tile):
        for m in range(8):
            ref[rows, 128 * m:128 * m + 128] = tile[128 * m:128 * m + 128, :]

    stage1()
    stage2_fixed()
    y_send_roots(1, *range(2 * CHUNKS))
    stage2()
    for kappa in range(2):
        @pl.when(c == roots[kappa])
        def _():
            for i in range(2):
                colv[kappa, i] = uvd[1, i] if kappa else uv[1, i, 1]

    def own_copy(kappa, i):
        return pltpu.make_async_copy(
            uvd.at[0, i] if kappa else uv.at[0, i, 1],
            left_out.at[i, kappa], own_sem.at[2 * kappa + i])
    for kappa in range(2):
        for i in range(2):
            @pl.when(c == roots[kappa])
            def _():
                own_copy(kappa, i).start()
    forward(1, 0)
    both(stage3_fixed)
    both(stage3)
    y_send_roots(0, 0)
    forward(1, 1)
    both(stage4_fixed)
    forward(1, 2)
    both(stage4)
    y_send_roots(0, 1, 2, 3, 4, 5)
    forward(1, 3, 4, 5)
    both(stage7, FIX)
    forward(0, 0)
    both(stage5)
    load_inv.wait()
    stage8(0, FIX)
    solve_main(0, t1, big_fu)
    both(stage7, OTH)
    forward(0, 1)
    both(stage7, CROSS)
    forward(0, 2)
    stage8(0, OTH)
    solve_main(1, t2, big_du)
    forward(0, 3, 4, 5)
    stage8(0, CROSS)
    same = step_row == step_col
    solve_cross(0, t1, jnp.where(same, 0, 1))
    solve_cross(1, t2, jnp.where(same, 1, 0))
    stage8(1, FIX)
    stage8(1, OTH)
    stage8(1, CROSS)
    y_finish(1)
    for col_k, cross_h, row_t, pm in ((step_col, 1 - step_col, t1, pm1), (1 - step_col, step_col, t2, pm2)):
        for i in range(2):
            unfold(vcat, slice(128 * i, 128 * i + 128), colv[col_k, i])
        unfold(vcat, slice(256, 384), bx_v[cross_h])
        prod = jnp.dot(vcat[...], solved[row_t], preferred_element_type=F32).astype(BF)
        for i in range(3):
            for j in range(3):
                pm[i, j] = prod[128 * i:128 * i + 128, 128 * j:128 * j + 128]

    def out_copy(i, j):
        return pltpu.make_async_copy(xout.at[i, j], x_hbm.at[i, j], out_sem.at[2 * i + j])

    one, zero = jnp.float32(1), jnp.float32(0)
    for j in range(2):
        jg = 2 * c + j
        col_live1 = jg != q1
        col_live2 = (jg != q1) & (jg != q2)
        right_f, right_d = big_fv[slot(j)], big_dv[slot(j)]
        unfold(rhs1, slice(0, 128), jnp.where(step_row == 0, right_f, right_d))
        unfold(rhs2, slice(0, 128), jnp.where(step_row == 0, right_d, right_f))
        h = (pm1[2, j].astype(F32) * jnp.where(col_live1, one, zero)).astype(BF)
        t_val = jnp.dot(h, rhs1[0:128, :], preferred_element_type=F32).astype(BF)
        rhs2[128:256, :] = t_val
        z_val = (jnp.dot(pm2[2, j], rhs2[0:128, :], preferred_element_type=F32)
                 - jnp.dot(pm2[2, 2], t_val, preferred_element_type=F32)).astype(BF)
        rhs1[128:256, :] = z_val
        for i in range(2):
            ig = 2 * r + i
            row_live1 = ig != p1
            m1 = jnp.where(row_live1 & col_live1, one, zero)
            m2 = jnp.where(row_live1 & (ig != p2) & col_live2, one, zero)
            band = slice(128 * i, 128 * i + 128)
            lhs1[band, 0:128] = (pm1[i, j].astype(F32) * -m1).astype(BF)
            lhs1[band, 128:256] = (pm1[i, 2].astype(F32) * m2).astype(BF)
            lhs2[band, 0:128] = (pm2[i, j].astype(F32) * -m2).astype(BF)
            lhs2[band, 128:256] = (pm2[i, 2].astype(F32) * m2).astype(BF)
        x1 = jnp.dot(lhs1[...], rhs1[...], preferred_element_type=F32).astype(BF)
        x2 = jnp.dot(lhs2[...], rhs2[...], preferred_element_type=F32).astype(BF)
        xf = jnp.where(step_col == 0, x1, x2)
        xd = jnp.where(step_col == 0, x2, x1)
        for i in range(2):
            xout[i, j, 0:128, :] = xf[128 * i:128 * i + 128]
            xout[i, j, 128:256, :] = xd[128 * i:128 * i + 128]
            out_copy(i, j).start()
    flush(row_pending)
    y_finish(0)
    for kappa in range(2):
        for i in range(2):
            @pl.when(c == roots[kappa])
            def _():
                own_copy(kappa, i).wait()
    for i in range(2):
        for j in range(2):
            out_copy(i, j).wait()
    flush(y_pending)


def exchange(root_d, order, ranks, tile_u, tile_v, inverses):
    def bf(*shape):
        return pltpu.VMEM(shape, BF)
    n_y = 8 * CHUNKS
    dma = pltpu.SemaphoreType.DMA
    any_spec = pl.BlockSpec(memory_space=pl.ANY)
    smem_spec = pl.BlockSpec(memory_space=pltpu.SMEM)
    return pl.pallas_call(
        functools.partial(comm_kernel, root_d),
        out_shape=(jax.ShapeDtypeStruct((2, 2, 1024, 128), BF), jax.ShapeDtypeStruct((2, 2, 256, 1024), BF)),
        in_specs=[smem_spec, smem_spec, any_spec, any_spec, any_spec],
        out_specs=(any_spec,) * 2,
        scratch_shapes=[
            bf(2, 2, 2, 1024, 128), bf(2, 2, 128, 1024), bf(2, 1024, 1024), bf(2, 2, 1024, 128), bf(2, 2, 1024, 128),
            bf(2, 2, 1024, 128), bf(2, 2, 1024, 128), bf(2, 2, 1024, 128), bf(4, 256, 128), bf(4, 256, 128),
            bf(2, 256, 128), bf(4, 256, 128), bf(4, 256, 128), bf(2, 256, 128)] + [bf(2, 1024, 128)] * 6 + [
            bf(1024, 256), bf(2, 1024, 384), bf(384, 1024), bf(3, 3, 128, 128), bf(3, 3, 128, 128),
            bf(256, 1024), bf(256, 1024), bf(256, 256), bf(256, 256), bf(2, 2, 256, 1024),
            dma((3,)), dma((4,)), dma((4,)), dma((3 * n_y,)), dma((n_y,)), dma((2, 36)), dma((2, 36))],
        compiler_params=pltpu.CompilerParams(
            collective_id=root_d, has_side_effects=True, vmem_limit_bytes=27 << 20),
        name="pivots_%d" % root_d,
    )(order, ranks, tile_u, tile_v, inverses)


def form_kernel(ranks_ref, cu_ref, x_ref, u_hbm, v_hbm, o_hbm, u, v, first, tiles, in_sem, out_sem):
    order = [(i, j) for i in range(2) for j in range(2)]
    loads = []
    for n, (i, j) in enumerate(order):
        loads.append((pltpu.make_async_copy(v_hbm.at[i, j], v.at[i, j], in_sem.at[2 * n]),
                      pltpu.make_async_copy(u_hbm.at[i, j], u.at[i, j], in_sem.at[2 * n + 1])))
        for load in loads[n]:
            load.start()

    def pivots(i, j, rows):
        left = jnp.concatenate([cu_ref[i, 0, rows, :], cu_ref[i, 1, rows, :]], 1)
        return jnp.dot(left, x_ref[i, j], preferred_element_type=F32)

    chunks = [pl.ds(FORM_ROWS * k, FORM_ROWS) for k in range(1024 // FORM_ROWS)]
    for rows in chunks:
        first[rows, :] = pivots(0, 0, rows)
    depth = lax.broadcasted_iota(jnp.int32, v.shape[2:], 0)
    copies = []
    for n, (i, j) in enumerate(order):
        for load in loads[n]:
            load.wait()
        right = jnp.where(depth < ranks_ref[i, j], v[i, j], jnp.zeros_like(v[i, j]))
        for rows in chunks:
            part = first[rows, :] if n == 0 else pivots(i, j, rows)
            own = jnp.dot(u[i, j, rows, :], right, preferred_element_type=F32)
            tiles[i, j, rows, :] = (part + own).astype(BF)
            copy = pltpu.make_async_copy(tiles.at[i, j, rows, :], o_hbm.at[i, j, rows, :], out_sem.at[len(copies)])
            copy.start()
            copies.append(copy)
    for copy in copies:
        copy.wait()


def form(ranks, tile_u, tile_v, col_u, right):
    shape = (2, 2, 1024, 1024)
    vmem, hbm = pl.BlockSpec(memory_space=pltpu.VMEM), pl.BlockSpec(memory_space=pl.ANY)
    return pl.pallas_call(
        form_kernel,
        out_shape=jax.ShapeDtypeStruct(shape, BF),
        in_specs=[pl.BlockSpec(memory_space=pltpu.SMEM), vmem, vmem, hbm, hbm],
        out_specs=hbm,
        scratch_shapes=[pltpu.VMEM(tile_u.shape, BF), pltpu.VMEM(tile_v.shape, BF), pltpu.VMEM((1024, 1024), F32),
                        pltpu.VMEM(shape, BF), pltpu.SemaphoreType.DMA((8,)),
                        pltpu.SemaphoreType.DMA((4096 // FORM_ROWS,))],
        compiler_params=pltpu.CompilerParams(vmem_limit_bytes=20 << 20),
        name="form_tiles",
    )(ranks, col_u, right, tile_u, tile_v)


def on_device(tile_u, tile_v, tile_ranks, inverses, panel_order):
    other = jnp.clip(jnp.sum(panel_order, axis=0) - (2 * FIXED_COL + 1), 0, 2 * FIXED_COL + 1)[1]
    branches = [functools.partial(exchange, root_d) for root_d in range(NY)]
    col_u, right = lax.switch(
        lax.shift_right_logical(other, 1), branches, panel_order, tile_ranks, tile_u, tile_v, inverses)
    return form(tile_ranks, tile_u, tile_v, col_u, right)


def solution(mesh):
    placed = (P("row", "col", None, None), P("row", "col", None, None), P("row", "col"), P(), P())
    return jax.shard_map(
        on_device,
        mesh=mesh,
        in_specs=placed,
        out_specs=P("row", "col", None, None),
        check_vma=False,
    )
```
